256 devices in a mesh: energy: 16 (over z_lo, y, core), slab: 16 (over z_hi, x).
Axes of the slice: x: 4, y: 4, z: 8 (z_hi: 4, z_lo: 2; z = z_hi * 2 + z_lo), core: 2. Of those that a mesh axis runs over, the one named last changes fastest.
Arguments:
- energies: float32 [32], P('energy'), may hold values from 2 to 3
- hamiltonian: bfloat16 [16, 512, 512], P('slab'), may hold values from -0.125 to 0.125
- coupling: bfloat16 [16, 512, 512], P('slab'), may hold values from -0.09375 to 0.09375
- coulomb: bfloat16 [16, 512, 512], P('slab', 'energy'), may hold values from 0.19921875 to 1
- offsets: int32 [8], replicated, may hold values from -16 to 16
Outputs:
- green: float32 [32, 16, 512, 512], P('energy', 'slab')
- self_part: bfloat16 [32, 16, 512, 512], P('energy', 'slab')
The draws below stay inside these ranges and needn't reach their ends.
All inputs are finite; a program needn't handle non-finite values.
Results may differ from the reference program's by a relative error of at most 0.0058.
Values may be sent and summed in bfloat16 or wider, within the bound.
No kernel may reach another device: no remote copies, remote signals or barrier semaphores. Data moves between devices by JAX's collectives and lax.ppermute only.
A program may use at most 64 MiB of HBM per device.

```python
import jax
import jax.numpy as jnp
from jax import lax

K = 512
NW = 8
ROUNDS = 2
PASSES = 2
NE = 32
NB = 16


def set_ends(values, own_key, smallest, largest):
    shape = values.shape
    place = [jax.random.randint(jax.random.fold_in(own_key, axis), (), 0, shape[axis]) for axis in range(len(shape))]
    values = values.at[tuple(place)].set(smallest)
    longest = shape.index(max(shape))
    place[longest] = (place[longest] + 1) % shape[longest]
    return values.at[tuple(place)].set(largest)


def block_levels(rng, dims, split, low, top_value):
    def one(axis_at, shards_of):
        heights = jax.random.uniform(jax.random.fold_in(jax.random.fold_in(rng, 6), axis_at), (shards_of,), jnp.float32, low / len(split), top_value / len(split))
        return jnp.repeat(jnp.exp(heights), dims[axis_at] // shards_of).reshape((-1,) + (1,) * (len(dims) - axis_at - 1))

    loudness = one(*split[0])
    for cut in split[1:]:
        loudness = loudness * one(*cut)
    return loudness


def bell_draw(own_key, extent, spread, limit, split=(), kind=jnp.bfloat16):
    array = jax.random.normal(own_key, extent, jnp.float32) * spread
    if len(split) > 0:
        array = block_levels(own_key, extent, split, -0.22, 0.18) * array
    return jnp.clip(array, min=-limit, max=limit).astype(kind)


def setup_inputs(seed: int = 0) -> dict:
    key_list = jax.random.split(jax.random.key(seed), 6)
    energies = jnp.clip(2.0 + 1.0 * jax.random.uniform(key_list[0], (NE,), jnp.float32) ** block_levels(key_list[0], (NE,), ((0, 16),), -0.2, 0.2), 2.0, 3.0)
    hamiltonian = bell_draw(key_list[1], (NB, K, K), (4 * K) ** -0.5, 0.125, ((0, 16),))
    coupling = bell_draw(key_list[2], (NB, K, K), (8 * K) ** -0.5, 0.09375, ((0, 16),))
    coulomb = jnp.clip(0.19921875 + 0.80078125 * jax.random.uniform(key_list[3], (NB, K, K), jnp.float32) ** block_levels(key_list[3], (NB, K, K), ((0, 16), (1, 16)), -0.2, 0.2), 0.19921875, 1.0).astype(jnp.bfloat16)
    offsets = set_ends(jax.random.randint(key_list[4], (NW,), 0 - NE // 2, NE // 2 + 1), jax.random.fold_in(key_list[4], 1), 0 - NE // 2, (NE // 2 + 1) - 1).astype(jnp.int32)
    return {"energies": energies, "hamiltonian": hamiltonian, "coupling": coupling, "coulomb": coulomb, "offsets": offsets}


BROAD = 0.3


def unit_tables(matrix_order):
    row_index = lax.broadcasted_iota(jnp.int32, (matrix_order, matrix_order), 0)
    column_index = lax.broadcasted_iota(jnp.int32, (matrix_order, matrix_order), 1)
    half_order = matrix_order // 2
    identity = (row_index == column_index).astype(jnp.float32)
    rotate = jnp.where((row_index < half_order) & (column_index == row_index + half_order), -1.0, 0.0) + jnp.where((row_index >= half_order) & (column_index == row_index - half_order), 1.0, 0.0)
    return identity, rotate.astype(jnp.float32)


def to_bfloat(values):
    return lax.optimization_barrier(values.astype(jnp.bfloat16)).astype(jnp.float32)


def newton_step(iterate, self_part, energy, hamiltonian, coupling, identity, rotate):
    highest = lax.Precision.HIGHEST
    green_wide = iterate.astype(jnp.bfloat16).astype(jnp.float32)
    links = coupling.astype(jnp.float32)
    above_block = jnp.concatenate([green_wide[1:], jnp.zeros_like(green_wide[:1])], 0)
    right_term = to_bfloat(jnp.einsum('bij,bkj->bik', above_block, links, precision=highest))
    upper_term = jnp.einsum('bij,bjk->bik', links, right_term, precision=highest)
    inner_term = to_bfloat(jnp.einsum('bij,bjk->bik', green_wide, links, precision=highest))
    own_term = to_bfloat(jnp.einsum('bji,bjk->bik', links, inner_term, precision=highest))
    lower_term = jnp.concatenate([jnp.zeros_like(own_term[:1]), own_term[:-1]], 0)
    base_matrix = energy * identity + BROAD * rotate - hamiltonian.astype(jnp.float32)
    matrix = base_matrix - self_part.astype(jnp.float32) - upper_term - lower_term
    product = jnp.einsum('bij,bjk->bik', to_bfloat(matrix), green_wide, precision=highest)
    residue = to_bfloat(2.0 * identity - product)
    return jnp.einsum('bij,bjk->bik', green_wide, residue, precision=highest)


def pick_energies(values, positions):
    inside = (positions >= 0) & (positions < values.shape[0])
    clipped = jnp.clip(positions, 0, values.shape[0] - 1).astype(jnp.int32)
    return jnp.where(inside[:, None, None], values[clipped], 0.0)


def self_energy(green_half, coulomb, offsets):
    energy_count = green_half.shape[0]
    offset_count = offsets.shape[0]
    levels = jnp.arange(energy_count, dtype=jnp.int32)

    def per_block(packed):
        block_green, weights = packed
        values = block_green.astype(jnp.float32)
        strength = weights.astype(jnp.float32)
        running = jnp.zeros_like(values)
        for number in range(offset_count):
            offset_now = offsets[number]
            later_green = pick_energies(values, levels + offset_now)
            polarization = (4.0 / energy_count) * jnp.sum(values * later_green, axis=0)
            screened = strength * (1.0 + polarization * strength)
            running = running + screened[None] * pick_energies(values, levels - offset_now)
        return (running / offset_count).astype(jnp.bfloat16)

    result = lax.map(per_block, (jnp.moveaxis(green_half, 1, 0), coulomb))
    return jnp.moveaxis(result, 0, 1)


def reference(energies, hamiltonian, coupling, coulomb, offsets):
    energy_count = energies.shape[0]
    block_count, matrix_order = hamiltonian.shape[0], hamiltonian.shape[1]
    identity, rotate = unit_tables(matrix_order)
    green = jnp.broadcast_to(identity[None, None] / energies[:, None, None, None], (energy_count, block_count, matrix_order, matrix_order))
    self_part = jnp.zeros((energy_count, block_count, matrix_order, matrix_order), jnp.bfloat16)

    def per_energy(packed):
        return newton_step(packed[0], packed[1], packed[2], hamiltonian, coupling, identity, rotate)

    for round_index in range(ROUNDS):
        for pass_index in range(PASSES):
            green = lax.map(per_energy, (green, self_part, energies))
        self_part = self_energy(green.astype(jnp.bfloat16), coulomb, offsets)
    return green, self_part
```

```python
import functools

import jax
import jax.numpy as jnp
from jax import lax
from jax.experimental import pallas as pl
from jax.experimental.pallas import tpu as pltpu
from jax.sharding import PartitionSpec as P

BROAD = 0.3
REACH = 16

VM = pl.BlockSpec(memory_space=pltpu.VMEM)
SM = pl.BlockSpec(memory_space=pltpu.SMEM)


def passed_along(value, axis, steps):
    count = lax.axis_size(axis)
    leading, last = (max(0, -steps), min(count, count - steps))
    return lax.ppermute(value, axis, [(source, source + steps) for source in range(leading, last)])


def call(body, out_shape, in_specs, scratch=()):
    return pl.pallas_call(
        body,
        out_shape=out_shape,
        in_specs=in_specs,
        out_specs=jax.tree.map(lambda _: VM, out_shape),
        scratch_shapes=list(scratch),
        compiler_params=pltpu.CompilerParams(vmem_limit_bytes=56 * 1024 * 1024),
    )


def dot(a, b):
    return jnp.dot(a, b, preferred_element_type=jnp.float32)


def dot_t(a, b):
    return lax.dot_general(a, b, (((1,), (1,)), ((), ())), preferred_element_type=jnp.float32)


def tables(n):
    row = lax.broadcasted_iota(jnp.int32, (n, n), 0)
    col = lax.broadcasted_iota(jnp.int32, (n, n), 1)
    half = n // 2
    eye = jnp.where(row == col, 1.0, 0.0)
    rotate = jnp.where(col == row + half, -1.0, 0.0) + jnp.where(col == row - half, 1.0, 0.0)
    return eye, rotate


def own_body(keep_ref, c_ref, own_ref):
    own_ref[...] = dot_t(c_ref[...], c_ref[...]) * keep_ref[0]


def pair_body(own_ref, below_ref, pair_ref, half_ref, turned_ref):
    turned = below_ref[...].T
    turned_ref[...] = turned
    pair = own_ref[...] + dot(turned, below_ref[...])
    pair_ref[...] = pair
    half_ref[...] = pair.astype(jnp.bfloat16)


def first_step(energy, inverse, ham, pair, eye, rotate):
    base = energy * eye + BROAD * rotate - ham.astype(jnp.float32)
    matrix = (base - inverse * pair.astype(jnp.float32)).astype(jnp.bfloat16).astype(jnp.float32)
    residue = (2.0 * eye - inverse * matrix).astype(jnp.bfloat16).astype(jnp.float32)
    return (inverse * residue).astype(jnp.bfloat16)


def neighbour_terms(above, below, c, lower_c, lower_turned):
    right = dot_t(above, c).astype(jnp.bfloat16)
    inner = dot(below, lower_c).astype(jnp.bfloat16)
    return dot(c, right) + dot(lower_turned, inner).astype(jnp.bfloat16).astype(jnp.float32)


def finish(matrix, green, eye):
    product = dot(matrix, green)
    residue = (2.0 * eye - product).astype(jnp.bfloat16)
    return dot(green, residue)


def second_body(
    energy_ref, inverse_ref, edge_ref, ham_ref, ham_up_ref, ham_down_ref, pair_ref, pair_up_ref, pair_down_ref,
    c_ref, lower_c_ref, lower_turned_ref, out_ref,
):
    n = c_ref.shape[0]
    eye, rotate = tables(n)
    chunks = out_ref.shape[0]
    for e in range(2):
        energy, inverse = energy_ref[e], inverse_ref[e]
        above = first_step(energy, inverse * edge_ref[0], ham_up_ref[...], pair_up_ref[...], eye, rotate)
        below = first_step(energy, inverse * edge_ref[1], ham_down_ref[...], pair_down_ref[...], eye, rotate)
        green = first_step(energy, inverse, ham_ref[...], pair_ref[...], eye, rotate)
        terms = neighbour_terms(above, below, c_ref[...], lower_c_ref[...], lower_turned_ref[...])
        base = energy * eye + BROAD * rotate - ham_ref[...].astype(jnp.float32)
        matrix = (base - terms).astype(jnp.bfloat16)
        result = finish(matrix, green, eye).astype(jnp.bfloat16)
        out_ref[:, e] = result.reshape(chunks, n // chunks, n)


def terms_body(energy_ref, ham_ref, up_ref, down_ref, c_ref, lower_c_ref, lower_turned_ref, out_ref):
    n = c_ref.shape[0]
    eye, rotate = tables(n)
    for e in range(2):
        terms = neighbour_terms(
            up_ref[:, e].reshape(n, n), down_ref[:, e].reshape(n, n), c_ref[...], lower_c_ref[...],
            lower_turned_ref[...],
        )
        base = energy_ref[e] * eye + BROAD * rotate - ham_ref[...].astype(jnp.float32)
        out_ref[e] = base - terms


def third_body(open_ref, self_ref, green_ref, out_ref):
    n = open_ref.shape[1]
    eye, _ = tables(n)
    for e in range(2):
        self_part = self_ref[:, e].reshape(n, n).astype(jnp.float32)
        matrix = (open_ref[e] - self_part).astype(jnp.bfloat16)
        out_ref[e] = finish(matrix, green_ref[:, e].reshape(n, n), eye).astype(jnp.bfloat16)


def fourth_body(
    energy_ref, ham_ref, up_ref, down_ref, c_ref, lower_c_ref, lower_turned_ref, self_ref, green_ref,
    wide_ref, out_ref,
):
    n = c_ref.shape[0]
    eye, rotate = tables(n)
    chunks = out_ref.shape[0]
    for e in range(2):
        terms = neighbour_terms(up_ref[e], down_ref[e], c_ref[...], lower_c_ref[...], lower_turned_ref[...])
        base = energy_ref[e] * eye + BROAD * rotate - ham_ref[...].astype(jnp.float32)
        self_part = self_ref[:, e].reshape(n, n).astype(jnp.float32)
        matrix = (base - self_part - terms).astype(jnp.bfloat16)
        result = finish(matrix, green_ref[e], eye)
        wide_ref[e] = result
        out_ref[:, e] = result.astype(jnp.bfloat16).reshape(chunks, n // chunks, n)


def energy_body(offset_ref, green_ref, coulomb_ref, out_ref, padded, wide):
    count, rows, columns = green_ref.shape
    offset_count = offset_ref.shape[0]
    none = jnp.zeros((REACH, rows, columns), jnp.float32)
    padded[:REACH] = none
    padded[REACH + count :] = none
    padded[REACH : REACH + count] = green_ref[...].astype(jnp.float32)
    wide[...] = coulomb_ref[...].astype(jnp.float32)
    column_tiles = columns // 128

    def tile(t, carry):
        place = (pl.ds(pl.multiple_of(8 * (t // column_tiles), 8), 8), pl.ds(pl.multiple_of(128 * (t % column_tiles), 128), 128))
        strength = wide[place]
        own = [padded[(REACH + e,) + place] for e in range(count)]
        screened = []
        for k in range(offset_count):
            shift = REACH + offset_ref[k]
            sums = [None] * 4
            for e in range(count):
                term = own[e] * padded[(shift + e,) + place]
                sums[e % 4] = term if sums[e % 4] is None else sums[e % 4] + term
            polarization = (4.0 / count) * ((sums[0] + sums[1]) + (sums[2] + sums[3]))
            screened.append(strength * (1.0 + polarization * strength) * (1.0 / offset_count))
        shifts = [REACH - offset_ref[k] for k in range(offset_count)]
        for e in range(count):
            total = screened[0] * padded[(shifts[0] + e,) + place]
            for k in range(1, offset_count):
                total = total + screened[k] * padded[(shifts[k] + e,) + place]
            out_ref[(e,) + place] = total.astype(jnp.bfloat16)
        return carry

    lax.fori_loop(0, (rows // 8) * column_tiles, tile, 0)


def self_energy(chunks, coulomb, offsets):
    parts, per, rows, columns = chunks.shape
    received = lax.all_to_all(chunks, "energy", split_axis=0, concat_axis=0, tiled=True)
    count = parts * per
    result = call(
        energy_body,
        jax.ShapeDtypeStruct((count, rows, columns), jnp.bfloat16),
        [SM, VM, VM],
        [pltpu.VMEM((count + 2 * REACH, rows, columns), jnp.float32), pltpu.VMEM((rows, columns), jnp.float32)],
    )(offsets, received.reshape(count, rows, columns), coulomb)
    return lax.all_to_all(
        result.reshape(parts, per, rows, columns), "energy", split_axis=0, concat_axis=0, tiled=True
    )


def local(energies, hamiltonian, coupling, coulomb, offsets):
    c, ham = coupling[0], hamiltonian[0]
    n = c.shape[0]
    parts = lax.axis_size("energy")
    place = lax.axis_index("slab")
    has_above = (place < lax.axis_size("slab") - 1).astype(jnp.float32)
    has_below = (place > 0).astype(jnp.float32)
    edge = jnp.stack([has_above, has_below])
    inverse = (1.0 / energies).astype(jnp.bfloat16).astype(jnp.float32)
    square = lambda kind: jax.ShapeDtypeStruct((n, n), kind)

    lower_c = passed_along(c, "slab", 1)
    ham_up = passed_along(ham, "slab", -1)
    ham_down = passed_along(ham, "slab", 1)
    own = call(own_body, square(jnp.float32), [SM, VM])(edge[:1], c)
    pair, pair_half, lower_turned = call(
        pair_body, (square(jnp.float32), square(jnp.bfloat16), square(jnp.bfloat16)), [VM, VM]
    )(own, lower_c)
    pair_up = passed_along(pair_half, "slab", -1)
    pair_down = passed_along(pair_half, "slab", 1)
    packed = jax.ShapeDtypeStruct((parts, 2, n // parts, n), jnp.bfloat16)
    green = call(second_body, packed, [SM] * 3 + [VM] * 9)(
        energies, inverse, edge, ham, ham_up, ham_down, pair, pair_up, pair_down, c, lower_c, lower_turned
    )
    up = passed_along(green, "slab", -1)
    down = passed_along(green, "slab", 1)
    open_part = call(terms_body, jax.ShapeDtypeStruct((2, n, n), jnp.float32), [SM] + [VM] * 6)(
        energies, ham, up, down, c, lower_c, lower_turned
    )
    self_part = self_energy(green, coulomb[0], offsets)
    green = call(third_body, jax.ShapeDtypeStruct((2, n, n), jnp.bfloat16), [VM] * 3)(open_part, self_part, green)
    up = passed_along(green, "slab", -1)
    down = passed_along(green, "slab", 1)
    wide, green = call(fourth_body, (jax.ShapeDtypeStruct((2, n, n), jnp.float32), packed), [SM] + [VM] * 8)(
        energies, ham, up, down, c, lower_c, lower_turned, self_part, green
    )
    self_part = self_energy(green, coulomb[0], offsets)
    self_part = jnp.swapaxes(self_part, 0, 1).reshape(2, n, n)
    return (wide[:, None], self_part[:, None])


def solution(mesh):
    placed = (
        P("energy"),
        P("slab", None, None),
        P("slab", None, None),
        P("slab", "energy", None),
        P(),
    )
    return jax.shard_map(
        local,
        mesh=mesh,
        in_specs=placed,
        out_specs=(P("energy", "slab", None, None), P("energy", "slab", None, None)),
        check_vma=False,
    )
```

```python
import functools

import jax
import jax.numpy as jnp
from jax import lax
from jax.experimental import pallas as pl
from jax.experimental.pallas import tpu as pltpu
from jax.sharding import PartitionSpec as P


BROAD = 0.3
REACH = 16

VM = pl.BlockSpec(memory_space=pltpu.VMEM)
SM = pl.BlockSpec(memory_space=pltpu.SMEM)


def passed_along(value, axis, steps):
    count = lax.axis_size(axis)
    leading, last = (max(0, -steps), min(count, count - steps))
    return lax.ppermute(value, axis, [(source, source + steps) for source in range(leading, last)])


def call(body, out_shape, in_specs, scratch=()):
    return pl.pallas_call(
        body,
        out_shape=out_shape,
        in_specs=in_specs,
        out_specs=jax.tree.map(lambda _: VM, out_shape),
        scratch_shapes=list(scratch),
        compiler_params=pltpu.CompilerParams(vmem_limit_bytes=56 * 1024 * 1024),
    )


def dot(a, b):
    return jnp.dot(a, b, preferred_element_type=jnp.float32)


def dot_t(a, b):
    return lax.dot_general(a, b, (((1,), (1,)), ((), ())), preferred_element_type=jnp.float32)


def tables(n):
    row = lax.broadcasted_iota(jnp.int32, (n, n), 0)
    col = lax.broadcasted_iota(jnp.int32, (n, n), 1)
    half = n // 2
    eye = jnp.where(row == col, 1.0, 0.0)
    rotate = jnp.where(col == row + half, -1.0, 0.0) + jnp.where(col == row - half, 1.0, 0.0)
    return eye, rotate


def own_body(keep_ref, c_ref, own_ref):
    own_ref[...] = dot_t(c_ref[...], c_ref[...]) * keep_ref[0]


def place_halves(core, whole, mine, theirs):
    half = mine.shape[0]
    whole[pl.ds(pl.multiple_of(core * half, half), half)] = mine
    whole[pl.ds(pl.multiple_of((1 - core) * half, half), half)] = theirs


def pair_body(core_ref, own_ref, mine_ref, theirs_ref, pair_ref, half_ref, below_ref, turned_ref):
    core = core_ref[0]
    half = half_ref.shape[0]
    place_halves(core, below_ref, mine_ref[...], theirs_ref[...])
    below = below_ref[...]
    turned = below.T
    turned_ref[...] = turned
    pair_ref[...] = own_ref[...] + dot(turned, below)
    half_ref[...] = pair_ref[pl.ds(pl.multiple_of(core * half, half), half)].astype(jnp.bfloat16)


def first_step(energy, inverse, ham, pair, eye, rotate):
    base = energy * eye + BROAD * rotate - ham.astype(jnp.float32)
    matrix = (base - inverse * pair.astype(jnp.float32)).astype(jnp.bfloat16).astype(jnp.float32)
    residue = (2.0 * eye - inverse * matrix).astype(jnp.bfloat16).astype(jnp.float32)
    return (inverse * residue).astype(jnp.bfloat16)


def neighbour_terms(above, below, c, lower_c, lower_turned):
    right = dot_t(above, c).astype(jnp.bfloat16)
    inner = dot(below, lower_c).astype(jnp.bfloat16)
    return dot(c, right) + dot(lower_turned, inner)


def finish(matrix, green, eye):
    product = dot(matrix, green)
    residue = (2.0 * eye - product).astype(jnp.bfloat16)
    return dot(green, residue)


def second_body(
    energy_ref, inverse_ref, edge_ref, core_ref, ham_ref, pair_ref, mine_ref, theirs_ref, c_ref, lower_c_ref,
    lower_turned_ref, out_ref, first_ref, second_ref, whole,
):
    n = c_ref.shape[0]
    eye, rotate = tables(n)
    chunks = out_ref.shape[0]
    for i in range(4):
        place_halves(core_ref[0], whole.at[i], mine_ref[i], theirs_ref[i])
    for e in range(2):
        energy, inverse = energy_ref[e], inverse_ref[e]
        above = first_step(energy, inverse * edge_ref[0], whole[0], whole[2], eye, rotate)
        below = first_step(energy, inverse * edge_ref[1], whole[1], whole[3], eye, rotate)
        green = first_step(energy, inverse, ham_ref[...], pair_ref[...], eye, rotate)
        terms = neighbour_terms(above, below, c_ref[...], lower_c_ref[...], lower_turned_ref[...])
        base = energy * eye + BROAD * rotate - ham_ref[...].astype(jnp.float32)
        matrix = (base - terms).astype(jnp.bfloat16)
        result = finish(matrix, green, eye).astype(jnp.bfloat16)
        out_ref[:, e] = result.reshape(chunks, n // chunks, n)
        (first_ref, second_ref)[e][...] = result


def terms_body(e, energy_ref, ham_ref, up_ref, down_ref, c_ref, lower_c_ref, lower_turned_ref, out_ref):
    eye, rotate = tables(c_ref.shape[0])
    terms = neighbour_terms(up_ref[...], down_ref[...], c_ref[...], lower_c_ref[...], lower_turned_ref[...])
    base = energy_ref[e] * eye + BROAD * rotate - ham_ref[...].astype(jnp.float32)
    out_ref[...] = base - terms


def third_body(e, open_ref, self_ref, green_ref, out_ref):
    n = open_ref.shape[0]
    eye, _ = tables(n)
    self_part = self_ref[:, e].reshape(n, n).astype(jnp.float32)
    matrix = (open_ref[...] - self_part).astype(jnp.bfloat16)
    out_ref[...] = finish(matrix, green_ref[...], eye).astype(jnp.bfloat16)


def fourth_body(
    e, energy_ref, ham_ref, up_ref, down_ref, c_ref, lower_c_ref, lower_turned_ref, self_ref, green_ref,
    wide_ref, out_ref,
):
    n = c_ref.shape[0]
    eye, rotate = tables(n)
    terms = neighbour_terms(up_ref[...], down_ref[...], c_ref[...], lower_c_ref[...], lower_turned_ref[...])
    base = energy_ref[e] * eye + BROAD * rotate - ham_ref[...].astype(jnp.float32)
    self_part = self_ref[:, e].reshape(n, n).astype(jnp.float32)
    matrix = (base - self_part - terms).astype(jnp.bfloat16)
    result = finish(matrix, green_ref[...], eye)
    wide_ref[...] = result
    out_ref[...] = result.astype(jnp.bfloat16)


def energy_body(offset_ref, green_ref, coulomb_ref, out_ref, padded, wide):
    count, rows, columns = green_ref.shape
    offset_count = offset_ref.shape[0]
    none = jnp.zeros((REACH, rows, columns), jnp.float32)
    padded[:REACH] = none
    padded[REACH + count :] = none
    padded[REACH : REACH + count] = green_ref[...].astype(jnp.float32)
    wide[...] = coulomb_ref[...].astype(jnp.float32)
    column_tiles = columns // 128

    def tile(t, carry):
        row = pl.ds(pl.multiple_of(8 * (t // column_tiles), 8), 8)
        column = pl.ds(pl.multiple_of(128 * (t % column_tiles), 128), 128)
        strength = wide[row, column]
        own = padded[REACH : REACH + count, row, column]
        total = jnp.zeros(own.shape, jnp.float32)
        screened = []
        for k in range(offset_count):
            later = padded[pl.ds(REACH + offset_ref[k], count), row, column]
            polarization = (4.0 / count) * jnp.sum(own * later, axis=0)
            screened.append(strength * (1.0 + polarization * strength) * (1.0 / offset_count))
        for k in range(offset_count):
            total = total + screened[k][None] * padded[pl.ds(REACH - offset_ref[k], count), row, column]
        out_ref[:, row, column] = total.astype(jnp.bfloat16)
        return carry

    lax.fori_loop(0, (rows // 8) * column_tiles, tile, 0)


def self_energy(chunks, coulomb, offsets):
    parts, per, rows, columns = chunks.shape
    received = lax.all_to_all(chunks, "energy", split_axis=0, concat_axis=0, tiled=True)
    count = parts * per
    result = call(
        energy_body,
        jax.ShapeDtypeStruct((count, rows, columns), jnp.bfloat16),
        [SM, VM, VM],
        [pltpu.VMEM((count + 2 * REACH, rows, columns), jnp.float32), pltpu.VMEM((rows, columns), jnp.float32)],
    )(offsets, received.reshape(count, rows, columns), coulomb)
    return lax.all_to_all(result.reshape(parts, per, rows, columns), "energy", split_axis=0, concat_axis=0, tiled=True)


WIDTH = 4


def row_hop(value, step):
    count = lax.axis_size("slab")
    start = WIDTH - 1 if step > 0 else WIDTH
    pairs = [(s, s + step * WIDTH) for s in range(start, count, WIDTH) if 0 <= s + step * WIDTH < count]
    return lax.ppermute(value, "slab", pairs)


def row_ring(value, hopped, step):
    count = lax.axis_size("slab")
    pairs = [(s, s // WIDTH * WIDTH + (s + step) % WIDTH) for s in range(count)]
    end = lax.axis_index("slab") % WIDTH == (WIDTH - 1 if step > 0 else 0)
    return lax.ppermute(jnp.where(end, hopped, value), "slab", pairs)


def swapped(value):
    count = lax.axis_size("energy")
    return lax.ppermute(value, "energy", [(s, s ^ 1) for s in range(count)])


def exchange(first, second):
    up_hop, down_hop = row_hop(first, -1), row_hop(first, 1)
    up_second, down_second = passed_along(second, "slab", -1), passed_along(second, "slab", 1)
    up_first, down_first = row_ring(first, up_hop, -1), row_ring(first, down_hop, 1)
    return (up_first, down_first), (up_second, down_second)


def whole_run(energies, hamiltonian, coupling, coulomb, offsets):
    c, ham = coupling[0], hamiltonian[0]
    n = c.shape[0]
    parts = lax.axis_size("energy")
    place = lax.axis_index("slab")
    has_above = (place < lax.axis_size("slab") - 1).astype(jnp.float32)
    has_below = (place > 0).astype(jnp.float32)
    edge = jnp.stack([has_above, has_below])
    core = lax.rem(lax.axis_index("energy"), 2)
    inverse = (1.0 / energies).astype(jnp.bfloat16).astype(jnp.float32)
    shape = lambda kind, *dims: jax.ShapeDtypeStruct(dims, kind)
    half = lambda value: lax.dynamic_slice_in_dim(value, core * (n // 2), n // 2, 0)
    wide, narrow = jnp.float32, jnp.bfloat16
    cores = core[None]

    lower_mine = passed_along(half(c), "slab", 1)
    ham_half = half(ham)
    ham_hop = row_hop(ham_half, 1)
    ham_up = passed_along(ham_half, "slab", -1)
    own = call(own_body, shape(wide, n, n), [SM, VM])(edge[:1], c)
    lower_theirs = swapped(lower_mine)
    pair, pair_half, lower_c, lower_turned = call(
        pair_body,
        (shape(wide, n, n), shape(narrow, n // 2, n), shape(narrow, n, n), shape(narrow, n, n)),
        [SM, VM, VM, VM],
    )(cores, own, lower_mine, lower_theirs)
    ham_down = row_ring(ham_half, ham_hop, 1)
    pair_up = passed_along(pair_half, "slab", -1)
    pair_down = passed_along(pair_half, "slab", 1)
    mine = jnp.stack([ham_up, ham_down, pair_up, pair_down])
    theirs = swapped(mine)
    packed = shape(narrow, parts, 2, n // parts, n)
    greens = call(
        second_body,
        (packed, shape(narrow, n, n), shape(narrow, n, n)),
        [SM] * 4 + [VM] * 7,
        [pltpu.VMEM((4, n, n), narrow)],
    )(energies, inverse, edge, cores, ham, pair, mine, theirs, c, lower_c, lower_turned)
    chunks, greens = greens[0], greens[1:]
    near = exchange(*greens)
    opened = [
        call(functools.partial(terms_body, e), shape(wide, n, n), [SM] + [VM] * 6)(
            energies, ham, *near[e], c, lower_c, lower_turned
        )
        for e in range(2)
    ]
    self_part = self_energy(chunks, coulomb[0], offsets)
    greens = [
        call(functools.partial(third_body, e), shape(narrow, n, n), [VM] * 3)(opened[e], self_part, greens[e])
        for e in range(2)
    ]
    near = exchange(*greens)
    last = [
        call(functools.partial(fourth_body, e), (shape(wide, n, n), shape(narrow, n, n)), [SM] + [VM] * 8)(
            energies, ham, *near[e], c, lower_c, lower_turned, self_part, greens[e]
        )
        for e in range(2)
    ]
    chunks = jnp.stack([last[e][1].reshape(parts, n // parts, n) for e in range(2)], 1)
    self_part = self_energy(chunks, coulomb[0], offsets)
    self_part = jnp.swapaxes(self_part, 0, 1).reshape(2, n, n)
    return (jnp.stack([last[0][0], last[1][0]])[:, None], self_part[:, None])


def solution(mesh):
    placed = (
        P("energy"),
        P("slab", None, None),
        P("slab", None, None),
        P("slab", "energy", None),
        P(),
    )
    return jax.shard_map(
        whole_run,
        mesh=mesh,
        in_specs=placed,
        out_specs=(P("energy", "slab", None, None), P("energy", "slab", None, None)),
        check_vma=False,
    )
```

```python
import functools

import jax
import jax.numpy as jnp
from jax import lax
from jax.experimental import pallas as pl
from jax.experimental.pallas import tpu as pltpu
from jax.sharding import PartitionSpec as P


BROAD = 0.3
REACH = 16

VM = pl.BlockSpec(memory_space=pltpu.VMEM)
SM = pl.BlockSpec(memory_space=pltpu.SMEM)


SLAB = ("row", "x")
ENERGY = ("zlo", "y", "core")
WIDTH = 4


def passed_along(value, steps):
    count = lax.axis_size(SLAB)
    leading, last = (max(0, -steps), min(count, count - steps))
    return lax.ppermute(value, SLAB, [(source, source + steps) for source in range(leading, last)])


def row_ring(value, steps):
    return lax.ppermute(value, "x", [(s, (s + steps) % WIDTH) for s in range(WIDTH)])


def row_climb(value):
    count = lax.axis_size(SLAB)
    return lax.ppermute(value, SLAB, [(s, s + WIDTH) for s in range(0, count - WIDTH, WIDTH)])


def swapped(value):
    return lax.ppermute(value, "core", [(0, 1), (1, 0)])


def row_above(value, both):
    rows = lax.axis_size("row")
    pairs = [(rows + r, r + 1) for r in range(rows - 1)]
    if both:
        pairs += [(r, rows + r - 1) for r in range(1, rows)]
    return lax.ppermute(value, ("core", "row"), pairs)


def flipped(value, side):
    pairs = [(c * WIDTH + i, (i // 2) * WIDTH + 2 * c + (i % 2 + side) % 2) for c in range(2) for i in range(WIDTH)]
    return lax.ppermute(value, ("core", "x"), pairs)


def call(body, out_shape, in_specs, scratch=()):
    return pl.pallas_call(
        body,
        out_shape=out_shape,
        in_specs=in_specs,
        out_specs=jax.tree.map(lambda _: VM, out_shape),
        scratch_shapes=list(scratch),
        compiler_params=pltpu.CompilerParams(vmem_limit_bytes=56 * 1024 * 1024),
    )


def dot(a, b):
    return jnp.dot(a, b, preferred_element_type=jnp.float32)


def dot_t(a, b):
    return lax.dot_general(a, b, (((1,), (1,)), ((), ())), preferred_element_type=jnp.float32)


def tables(n):
    row = lax.broadcasted_iota(jnp.int32, (n, n), 0)
    col = lax.broadcasted_iota(jnp.int32, (n, n), 1)
    half = n // 2
    eye = jnp.where(row == col, 1.0, 0.0)
    rotate = jnp.where(col == row + half, -1.0, 0.0) + jnp.where(col == row - half, 1.0, 0.0)
    return eye, rotate


def own_body(keep_ref, at_ref, c_ref, ham_ref, own_ref, load_ref):
    own_ref[...] = dot_t(c_ref[...], c_ref[...]) * keep_ref[0]
    load_ref[...] = jnp.where(at_ref[0] == 0, ham_ref[...], c_ref[...])


def place_halves(core, whole, mine, theirs):
    half = mine.shape[0]
    whole[pl.ds(pl.multiple_of(core * half, half), half)] = mine
    whole[pl.ds(pl.multiple_of((1 - core) * half, half), half)] = theirs


def pair_body(at_ref, own_ref, mine_ref, theirs_ref, pair_ref, half_ref, below_ref, turned_ref):
    core = at_ref[0]
    half = half_ref.shape[0]
    place_halves(core, below_ref, mine_ref[...], theirs_ref[...])
    below = below_ref[...]
    turned = below.T
    turned_ref[...] = turned
    pair_ref[...] = own_ref[...] + dot(turned, below)
    half_ref[...] = pair_ref[pl.ds(pl.multiple_of(core * half, half), half)].astype(jnp.bfloat16)


def first_step(energy, inverse, ham, pair, eye, rotate):
    base = energy * eye + BROAD * rotate - ham.astype(jnp.float32)
    matrix = (base - inverse * pair.astype(jnp.float32)).astype(jnp.bfloat16).astype(jnp.float32)
    residue = (2.0 * eye - inverse * matrix).astype(jnp.bfloat16).astype(jnp.float32)
    return (inverse * residue).astype(jnp.bfloat16)


def linked(green, link):
    return dot(link, dot_t(green, link).astype(jnp.bfloat16))


def finish(matrix, green, eye):
    product = dot(matrix, green)
    residue = (2.0 * eye - product).astype(jnp.bfloat16)
    return dot(green, residue)


def second_body(
    energy_ref, inverse_ref, edge_ref, at_ref, ham_ref, pair_ref, mine_ref, theirs_ref, c_ref, lower_turned_ref,
    out_ref, first_ref, second_ref, whole,
):
    n = c_ref.shape[0]
    eye, rotate = tables(n)
    chunks = out_ref.shape[0]
    for i in range(4):
        place_halves(at_ref[0], whole.at[i], mine_ref[i], theirs_ref[i])
    odd = lax.rem(at_ref[1], 2)
    for e, same_ref in ((odd, first_ref), (1 - odd, second_ref)):
        energy, inverse = energy_ref[e], inverse_ref[e]
        above = first_step(energy, inverse * edge_ref[0], whole[0], whole[2], eye, rotate)
        below = first_step(energy, inverse * edge_ref[1], whole[1], whole[3], eye, rotate)
        green = first_step(energy, inverse, ham_ref[...], pair_ref[...], eye, rotate)
        base = energy * eye + BROAD * rotate - ham_ref[...].astype(jnp.float32)
        matrix = (base - linked(above, c_ref[...]) - linked(below, lower_turned_ref[...])).astype(jnp.bfloat16)
        result = finish(matrix, green, eye).astype(jnp.bfloat16)
        out_ref[:, e] = result.reshape(chunks, n // chunks, n)
        same_ref[...] = result


def gather_body(at_ref, here_ref, one_ref, two_ref, three_ref, all_ref, give_ref, last_ref):
    core, x = at_ref[0], at_ref[1]
    for k, ref in enumerate((here_ref, one_ref, two_ref, three_ref)):
        all_ref[lax.rem(x + WIDTH - k, WIDTH)] = ref[...]
    give_ref[...] = all_ref[pl.ds(2 * (1 - core), 2)]
    last_ref[...] = all_ref[WIDTH - 1]


def link_body(at_ref, all_ref, got_ref, below_ref, outer_ham, inner_ham, far, mid, mid_turned, near):
    @pl.when(at_ref[0] == 0)
    def _():
        outer_ham[...] = all_ref[0]
        inner_ham[...] = all_ref[1]
        far[...] = below_ref[...].T
        mid[...] = got_ref[0]
        mid_turned[...] = got_ref[0].T
        near[...] = got_ref[1]

    @pl.when(at_ref[0] == 1)
    def _():
        outer_ham[...] = got_ref[1]
        inner_ham[...] = got_ref[0]
        far[...] = all_ref[3]
        mid[...] = all_ref[2].T
        mid_turned[...] = all_ref[2]
        near[...] = all_ref[1].T


def role_body(at_ref, first_ref, second_ref, outer_ref, inner_ref):
    match = lax.rem(at_ref[1], 2) == at_ref[0]
    outer_ref[...] = jnp.where(match, first_ref[...], second_ref[...])
    inner_ref[...] = jnp.where(match, second_ref[...], first_ref[...])


def open_body(
    energy_ref, outer_ham, inner_ham, far, mid, mid_turned, near, outer, inner, beyond, beside, open_outer, open_inner,
):
    eye, rotate = tables(outer.shape[0])
    base = energy_ref[0] * eye + BROAD * rotate
    open_outer[...] = (
        base - outer_ham[...].astype(jnp.float32) - linked(inner[...], mid[...]) - linked(beyond[...], far[...])
    )
    open_inner[...] = (
        base - inner_ham[...].astype(jnp.float32) - linked(outer[...], mid_turned[...]) - linked(beside[...], near[...])
    )


def joined_rows(core, slot, mine_ref, theirs_ref, scratch):
    scratch[:, core] = mine_ref[2 * core + slot]
    scratch[:, 1 - core] = theirs_ref[slot]
    n = scratch.shape[-1]
    return scratch[...].reshape(n, n).astype(jnp.float32)


def third_body(inner, at_ref, open_ref, mine_ref, theirs_ref, green_ref, out_ref, scratch):
    core = at_ref[0]
    eye, _ = tables(open_ref.shape[0])
    self_part = joined_rows(core, 1 - core if inner else core, mine_ref, theirs_ref, scratch)
    matrix = (open_ref[...] - self_part).astype(jnp.bfloat16)
    out_ref[...] = finish(matrix, green_ref[...], eye).astype(jnp.bfloat16)


def split_rows(core, result, keep_ref, give_ref, scratch):
    scratch[...] = result.reshape(scratch.shape)
    keep_ref[...] = scratch[:, core]
    give_ref[...] = scratch[:, 1 - core]


def inner_body(
    energy_ref, at_ref, outer_ham, inner_ham, mid, mid_turned, near, mine_ref, theirs_ref, outer, inner, beside,
    open_outer, whole_ref, keep_ref, give_ref, scratch,
):
    core = at_ref[0]
    eye, rotate = tables(outer.shape[0])
    base = energy_ref[0] * eye + BROAD * rotate
    self_part = joined_rows(core, 1 - core, mine_ref, theirs_ref, scratch)
    matrix = (
        base - inner_ham[...].astype(jnp.float32) - self_part - linked(outer[...], mid_turned[...])
        - linked(beside[...], near[...])
    ).astype(jnp.bfloat16)
    result = finish(matrix, inner[...], eye).astype(jnp.bfloat16)
    whole_ref[...] = result
    split_rows(core, result, keep_ref, give_ref, scratch)
    self_part = joined_rows(core, core, mine_ref, theirs_ref, scratch)
    open_outer[...] = base - outer_ham[...].astype(jnp.float32) - self_part - linked(inner[...], mid[...])


def outer_body(at_ref, far, open_ref, outer, beyond, whole_ref, keep_ref, give_ref, scratch):
    eye, _ = tables(outer.shape[0])
    matrix = (open_ref[...] - linked(beyond[...], far[...])).astype(jnp.bfloat16)
    result = finish(matrix, outer[...], eye).astype(jnp.bfloat16)
    whole_ref[...] = result
    split_rows(at_ref[0], result, keep_ref, give_ref, scratch)


def join_body(at_ref, keep_outer, keep_inner, got_outer, got_inner, out_ref):
    first = at_ref[0] == 0
    out_ref[0] = jnp.where(first, keep_outer[...], got_outer[...])
    out_ref[1] = jnp.where(first, keep_inner[...], got_inner[...])
    out_ref[2] = jnp.where(first, got_inner[...], keep_inner[...])
    out_ref[3] = jnp.where(first, got_outer[...], keep_outer[...])


def spread_body(at_ref, first_ref, second_ref, out_ref):
    odd = lax.rem(at_ref[1], 2)
    out_ref[odd] = first_ref[...].astype(jnp.float32)
    out_ref[1 - odd] = second_ref[...].astype(jnp.float32)


def energy_body(place_in, place_out, offset_ref, green_ref, coulomb_ref, out_ref, padded, wide):
    count, rows, columns = green_ref.shape
    offset_count = offset_ref.shape[0]
    none = jnp.zeros((REACH, rows, columns), jnp.float32)
    padded[:REACH] = none
    padded[REACH + count :] = none
    for e in range(count):
        padded[REACH + e] = green_ref[place_in[e]].astype(jnp.float32)
    wide[...] = coulomb_ref[...].astype(jnp.float32)
    column_tiles = columns // 128

    def tile(t, carry):
        row = pl.ds(pl.multiple_of(8 * (t // column_tiles), 8), 8)
        column = pl.ds(pl.multiple_of(128 * (t % column_tiles), 128), 128)
        strength = wide[row, column]
        own = padded[REACH : REACH + count, row, column]
        total = jnp.zeros(own.shape, jnp.float32)
        screened = []
        for k in range(offset_count):
            later = padded[pl.ds(REACH + offset_ref[k], count), row, column]
            polarization = (4.0 / count) * jnp.sum(own * later, axis=0)
            screened.append(strength * (1.0 + polarization * strength) * (1.0 / offset_count))
        for k in range(offset_count):
            total = total + screened[k][None] * padded[pl.ds(REACH - offset_ref[k], count), row, column]
        total = total.astype(jnp.bfloat16)
        for e in range(count):
            out_ref[place_out[e], row, column] = total[e]
        return carry

    lax.fori_loop(0, (rows // 8) * column_tiles, tile, 0)


def convolved(received, coulomb, offsets, place_in, place_out):
    count, rows, columns = received.shape
    return call(
        functools.partial(energy_body, place_in, place_out),
        jax.ShapeDtypeStruct((count, rows, columns), jnp.bfloat16),
        [SM, VM, VM],
        [pltpu.VMEM((count + 2 * REACH, rows, columns), jnp.float32), pltpu.VMEM((rows, columns), jnp.float32)],
    )(offsets, received, coulomb)


def all_to_all(value, axes):
    return lax.all_to_all(value, axes, split_axis=0, concat_axis=0, tiled=True)


def whole_run(energies, hamiltonian, coupling, coulomb, offsets):
    c, ham, strength = coupling[0], hamiltonian[0], coulomb[0]
    n = c.shape[0]
    parts = lax.axis_size(ENERGY)
    rows, pairs = n // parts, parts // 2
    count = 2 * parts
    place, x, core = lax.axis_index(SLAB), lax.axis_index("x"), lax.axis_index("core")
    edge = jnp.stack([place < lax.axis_size(SLAB) - 1, place > 0]).astype(jnp.float32)
    at = jnp.stack([core, x]).astype(jnp.int32)
    inverse = (1.0 / energies).astype(jnp.bfloat16).astype(jnp.float32)
    half = lambda value: lax.dynamic_slice_in_dim(value, core * (n // 2), n // 2, 0)
    wide = lambda *dims: jax.ShapeDtypeStruct(dims, jnp.float32)
    thin = lambda *dims: jax.ShapeDtypeStruct(dims, jnp.bfloat16)
    natural = list(range(count))
    by_chip = [(e % WIDTH) * (count // WIDTH) + e // WIDTH for e in range(count)]

    lower_mine = passed_along(half(c), 1)
    ham_half = half(ham)
    ham_ring = row_ring(ham_half, 1)
    ham_up = passed_along(ham_half, -1)
    energy_pair = swapped(energies)
    own, load = call(own_body, (wide(n, n), thin(n, n)), [SM, SM, VM, VM])(edge[:1], at, c, ham)
    lower_theirs = swapped(lower_mine)
    ham_climb = row_climb(ham_ring)
    pair, pair_half, _, lower_turned = call(
        pair_body, (wide(n, n), thin(n // 2, n), thin(n, n), thin(n, n)), [SM, VM, VM, VM]
    )(at, own, lower_mine, lower_theirs)
    pair_up = passed_along(pair_half, -1)
    pair_down = passed_along(pair_half, 1)
    mine = jnp.stack([ham_up, jnp.where(x == 0, ham_climb, ham_ring), pair_up, pair_down])
    theirs = swapped(mine)
    one, three = row_ring(load, 1), row_ring(load, -1)
    chunks, first, second = call(
        second_body,
        (thin(parts, 2, rows, n), thin(n, n), thin(n, n)),
        [SM] * 4 + [VM] * 6,
        [pltpu.VMEM((4, n, n), jnp.bfloat16)],
    )(energies, inverse, edge, at, ham, pair, mine, theirs, c, lower_turned)
    first, second = flipped(first, 0), flipped(second, 1)
    two = row_ring(one, 1)
    received = all_to_all(chunks, ENERGY)

    everything, give, last = call(gather_body, (thin(WIDTH, n, n), thin(2, n, n), thin(n, n)), [SM] + [VM] * 4)(
        at, load, one, two, three
    )
    got = swapped(give)
    below_c = row_above(last, False)
    outer_ham, inner_ham, far, mid, mid_turned, near = call(link_body, (thin(n, n),) * 6, [SM] + [VM] * 3)(
        at, everything, got, below_c
    )
    fours = jnp.where(core == 0, jnp.concatenate([energies, energy_pair]), jnp.concatenate([energy_pair, energies]))
    energy = lax.dynamic_slice_in_dim(fours, x, 1)
    outer, inner = call(role_body, (thin(n, n),) * 2, [SM, VM, VM])(at, first, second)
    beyond = row_above(outer, True)
    beside = swapped(inner)
    open_outer, open_inner = call(open_body, (wide(n, n),) * 2, [SM] + [VM] * 10)(
        energy, outer_ham, inner_ham, far, mid, mid_turned, near, outer, inner, beyond, beside
    )
    result = convolved(received.reshape(count, rows, n), strength, offsets, natural, by_chip)
    self_mine = all_to_all(result, ("x", "zlo", "y")).reshape(WIDTH, pairs, rows, n)
    self_theirs = swapped(lax.dynamic_slice_in_dim(self_mine, 2 * (1 - core), 2, 0))
    mix = [pltpu.VMEM((pairs, 2, rows, n), jnp.bfloat16)]
    third = lambda role, opened, green: call(
        functools.partial(third_body, role), thin(n, n), [SM] + [VM] * 4, mix
    )(at, opened, self_mine, self_theirs, green)
    outer = third(False, open_outer, outer)
    beyond = row_above(outer, True)
    inner = third(True, open_inner, inner)
    beside = swapped(inner)
    open_outer, whole_inner, keep_inner, give_inner = call(
        inner_body, (wide(n, n), thin(n, n), thin(pairs, rows, n), thin(pairs, rows, n)), [SM] * 2 + [VM] * 10, mix
    )(energy, at, outer_ham, inner_ham, mid, mid_turned, near, self_mine, self_theirs, outer, inner, beside)
    got_inner = swapped(give_inner)
    whole_outer, keep_outer, give_outer = call(
        outer_body, (thin(n, n), thin(pairs, rows, n), thin(pairs, rows, n)), [SM] + [VM] * 4, mix
    )(at, far, open_outer, outer, beyond)
    got_outer = swapped(give_outer)
    chunks = call(join_body, thin(WIDTH, pairs, rows, n), [SM] + [VM] * 4)(
        at, keep_outer, keep_inner, got_outer, got_inner
    )
    received = all_to_all(chunks.reshape(count, rows, n), ("x", "zlo", "y"))
    first, second = call(role_body, (thin(n, n),) * 2, [SM, VM, VM])(at, whole_outer, whole_inner)
    first, second = flipped(first, 0), flipped(second, 1)
    result = convolved(received, strength, offsets, by_chip, natural)
    self_part = all_to_all(result.reshape(parts, 2, rows, n), ENERGY)
    green = call(spread_body, wide(2, n, n), [SM, VM, VM])(at, first, second)
    self_part = jnp.swapaxes(self_part, 0, 1).reshape(2, n, n)
    return (green[:, None], self_part[:, None])


def fine_mesh(mesh):
    energy, slab = mesh.shape["energy"], mesh.shape["slab"]
    zlo, y = (2, energy // 4) if energy > 2 else (1, 1)
    devices = mesh.devices.reshape(zlo, y, 2, slab // WIDTH, WIDTH)
    return jax.sharding.Mesh(devices, ("zlo", "y", "core", "row", "x"))


def solution(mesh):
    mesh = fine_mesh(mesh)
    return jax.shard_map(
        whole_run,
        mesh=mesh,
        in_specs=(P(ENERGY), P(SLAB), P(SLAB), P(SLAB, ENERGY), P()),
        out_specs=(P(ENERGY, SLAB), P(ENERGY, SLAB)),
        check_vma=False,
    )
```

```python
import functools

import jax
import jax.numpy as jnp
from jax import lax
from jax.experimental import pallas as pl
from jax.experimental.pallas import tpu as pltpu
from jax.sharding import PartitionSpec as P


BROAD = 0.3
REACH = 16

VM = pl.BlockSpec(memory_space=pltpu.VMEM)
SM = pl.BlockSpec(memory_space=pltpu.SMEM)


SLAB = ("row", "x")
ENERGY = ("zlo", "y", "core")
WIDTH = 4


def passed_along(value, steps):
    count = lax.axis_size(SLAB)
    leading, last = (max(0, -steps), min(count, count - steps))
    return lax.ppermute(value, SLAB, [(source, source + steps) for source in range(leading, last)])


def row_ring(value, steps):
    return lax.ppermute(value, "x", [(s, (s + steps) % WIDTH) for s in range(WIDTH)])


def swapped(value):
    return lax.ppermute(value, "core", [(0, 1), (1, 0)])


def row_above(value, both):
    rows = lax.axis_size("row")
    pairs = [(rows + r, r + 1) for r in range(rows - 1)]
    if both:
        pairs += [(r, rows + r - 1) for r in range(1, rows)]
    return lax.ppermute(value, ("core", "row"), pairs)


def flipped(value, side):
    pairs = [(c * WIDTH + i, (i // 2) * WIDTH + 2 * c + (i % 2 + side) % 2) for c in range(2) for i in range(WIDTH)]
    return lax.ppermute(value, ("core", "x"), pairs)


def call(body, out_shape, in_specs, scratch=()):
    return pl.pallas_call(
        body,
        out_shape=out_shape,
        in_specs=in_specs,
        out_specs=jax.tree.map(lambda _: VM, out_shape),
        scratch_shapes=list(scratch),
        compiler_params=pltpu.CompilerParams(vmem_limit_bytes=56 * 1024 * 1024),
    )


def dot(a, b):
    return jnp.dot(a, b, preferred_element_type=jnp.float32)


def dot_t(a, b):
    return lax.dot_general(a, b, (((1,), (1,)), ((), ())), preferred_element_type=jnp.float32)


def tables(n):
    row = lax.broadcasted_iota(jnp.int32, (n, n), 0)
    col = lax.broadcasted_iota(jnp.int32, (n, n), 1)
    half = n // 2
    eye = jnp.where(row == col, 1.0, 0.0)
    rotate = jnp.where(col == row + half, -1.0, 0.0) + jnp.where(col == row - half, 1.0, 0.0)
    return eye, rotate


def own_body(keep_ref, at_ref, c_ref, ham_ref, own_ref, load_ref):
    own_ref[...] = dot_t(c_ref[...], c_ref[...]) * keep_ref[0]
    load_ref[...] = jnp.where(at_ref[0] == 0, ham_ref[...], c_ref[...])


def place_halves(core, whole, mine, theirs):
    half = mine.shape[0]
    whole[pl.ds(pl.multiple_of(core * half, half), half)] = mine
    whole[pl.ds(pl.multiple_of((1 - core) * half, half), half)] = theirs


def pair_body(at_ref, own_ref, mine_ref, theirs_ref, pair_ref, half_ref, below_ref, turned_ref):
    core = at_ref[0]
    half = half_ref.shape[0]
    place_halves(core, below_ref, mine_ref[...], theirs_ref[...])
    below = below_ref[...]
    turned = below.T
    turned_ref[...] = turned
    pair_ref[...] = own_ref[...] + dot(turned, below)
    half_ref[...] = pair_ref[pl.ds(pl.multiple_of(core * half, half), half)].astype(jnp.bfloat16)


def first_step(energy, inverse, ham, pair, eye, rotate):
    base = energy * eye + BROAD * rotate - ham.astype(jnp.float32)
    matrix = (base - inverse * pair.astype(jnp.float32)).astype(jnp.bfloat16).astype(jnp.float32)
    residue = (2.0 * eye - inverse * matrix).astype(jnp.bfloat16).astype(jnp.float32)
    return (inverse * residue).astype(jnp.bfloat16)


def linked(green, link):
    return dot(link, dot_t(green, link).astype(jnp.bfloat16))


def finish(matrix, green, eye):
    product = dot(matrix, green)
    residue = (2.0 * eye - product).astype(jnp.bfloat16)
    return dot(green, residue)


def second_body(
    energy_ref, inverse_ref, edge_ref, at_ref, ham_ref, pair_ref, c_ref, lower_turned_ref, *refs
):
    mine_refs, theirs_refs = refs[:4], refs[4:8]
    out_ref, first_ref, second_ref, whole = refs[8:]
    n = c_ref.shape[0]
    eye, rotate = tables(n)
    chunks = out_ref.shape[0]
    for i in range(4):
        place_halves(at_ref[0], whole.at[i], mine_refs[i][...], theirs_refs[i][...])
    odd = lax.rem(at_ref[1], 2)
    for e, same_ref in ((odd, first_ref), (1 - odd, second_ref)):
        energy, inverse = energy_ref[e], inverse_ref[e]
        above = first_step(energy, inverse * edge_ref[0], whole[0], whole[2], eye, rotate)
        below = first_step(energy, inverse * edge_ref[1], whole[1], whole[3], eye, rotate)
        green = first_step(energy, inverse, ham_ref[...], pair_ref[...], eye, rotate)
        base = energy * eye + BROAD * rotate - ham_ref[...].astype(jnp.float32)
        matrix = (base - linked(above, c_ref[...]) - linked(below, lower_turned_ref[...])).astype(jnp.bfloat16)
        result = finish(matrix, green, eye).astype(jnp.bfloat16)
        out_ref[:, e] = result.reshape(chunks, n // chunks, n)
        same_ref[...] = result


def gather_body(at_ref, here_ref, one_ref, two_ref, three_ref, all_ref, give_ref, last_ref):
    core, x = at_ref[0], at_ref[1]
    for k, ref in enumerate((here_ref, one_ref, two_ref, three_ref)):
        all_ref[lax.rem(x + WIDTH - k, WIDTH)] = ref[...]
    give_ref[...] = all_ref[pl.ds(2 * (1 - core), 2)]
    last_ref[...] = all_ref[WIDTH - 1]


def link_body(at_ref, all_ref, got_ref, below_ref, outer_ham, inner_ham, far, mid, mid_turned, near):
    @pl.when(at_ref[0] == 0)
    def _():
        outer_ham[...] = all_ref[0]
        inner_ham[...] = all_ref[1]
        far[...] = below_ref[...].T
        mid[...] = got_ref[0]
        mid_turned[...] = got_ref[0].T
        near[...] = got_ref[1]

    @pl.when(at_ref[0] == 1)
    def _():
        outer_ham[...] = got_ref[1]
        inner_ham[...] = got_ref[0]
        far[...] = all_ref[3]
        mid[...] = all_ref[2].T
        mid_turned[...] = all_ref[2]
        near[...] = all_ref[1].T


def row_energy(at_ref, energy_ref, pair_ref):
    core, x = at_ref[0], at_ref[1]
    return jnp.where(x // 2 == core, energy_ref[lax.rem(x, 2)], pair_ref[lax.rem(x, 2)])


def role_body(at_ref, first_ref, second_ref, outer_ref, inner_ref):
    match = lax.rem(at_ref[1], 2) == at_ref[0]
    outer_ref[...] = jnp.where(match, first_ref[...], second_ref[...])
    inner_ref[...] = jnp.where(match, second_ref[...], first_ref[...])


def open_body(
    at_ref, energy_ref, energy_pair_ref, outer_ham, inner_ham, far, mid, mid_turned, near, outer, inner, beyond, beside, open_outer, open_inner,
):
    eye, rotate = tables(outer.shape[0])
    base = row_energy(at_ref, energy_ref, energy_pair_ref) * eye + BROAD * rotate
    open_outer[...] = (
        base - outer_ham[...].astype(jnp.float32) - linked(inner[...], mid[...]) - linked(beyond[...], far[...])
    )
    open_inner[...] = (
        base - inner_ham[...].astype(jnp.float32) - linked(outer[...], mid_turned[...]) - linked(beside[...], near[...])
    )


def joined_rows(core, slot, mine_ref, theirs_ref, scratch):
    scratch[:, core] = mine_ref[2 * core + slot]
    scratch[:, 1 - core] = theirs_ref[slot]
    n = scratch.shape[-1]
    return scratch[...].reshape(n, n).astype(jnp.float32)


def third_body(inner, at_ref, open_ref, mine_ref, theirs_ref, green_ref, out_ref, scratch):
    core = at_ref[0]
    eye, _ = tables(open_ref.shape[0])
    self_part = joined_rows(core, 1 - core if inner else core, mine_ref, theirs_ref, scratch)
    matrix = (open_ref[...] - self_part).astype(jnp.bfloat16)
    out_ref[...] = finish(matrix, green_ref[...], eye).astype(jnp.bfloat16)


def split_rows(core, result, keep_ref, give_ref, scratch):
    scratch[...] = result.reshape(scratch.shape)
    keep_ref[...] = scratch[:, core]
    give_ref[...] = scratch[:, 1 - core]


def inner_body(
    at_ref, energy_ref, energy_pair_ref, outer_ham, inner_ham, mid, mid_turned, near, mine_ref, theirs_ref, outer, inner, beside,
    open_outer, whole_ref, keep_ref, give_ref, scratch,
):
    core = at_ref[0]
    eye, rotate = tables(outer.shape[0])
    base = row_energy(at_ref, energy_ref, energy_pair_ref) * eye + BROAD * rotate
    self_part = joined_rows(core, 1 - core, mine_ref, theirs_ref, scratch)
    matrix = (
        base - inner_ham[...].astype(jnp.float32) - self_part - linked(outer[...], mid_turned[...])
        - linked(beside[...], near[...])
    ).astype(jnp.bfloat16)
    result = finish(matrix, inner[...], eye).astype(jnp.bfloat16)
    whole_ref[...] = result
    split_rows(core, result, keep_ref, give_ref, scratch)
    self_part = joined_rows(core, core, mine_ref, theirs_ref, scratch)
    open_outer[...] = base - outer_ham[...].astype(jnp.float32) - self_part - linked(inner[...], mid[...])


def outer_body(
    at_ref, far, open_ref, outer, beyond, keep_inner, got_inner, whole_ref, out_ref, give_ref, scratch
):
    core = at_ref[0]
    eye, _ = tables(outer.shape[0])
    matrix = (open_ref[...] - linked(beyond[...], far[...])).astype(jnp.bfloat16)
    result = finish(matrix, outer[...], eye).astype(jnp.bfloat16)
    whole_ref[...] = result
    scratch[...] = result.reshape(scratch.shape)
    give_ref[...] = scratch[:, 1 - core]
    out_ref[3 * core] = scratch[:, core]
    out_ref[1 + core] = keep_inner[...]
    out_ref[2 - core] = got_inner[...]
    out_ref[3 - 3 * core] = got_inner[...]


def spread_body(at_ref, first_ref, second_ref, out_ref):
    odd = lax.rem(at_ref[1], 2)
    out_ref[odd] = first_ref[...].astype(jnp.float32)
    out_ref[1 - odd] = second_ref[...].astype(jnp.float32)


def energy_body(place_in, place_out, offset_ref, green_ref, coulomb_ref, out_ref, padded, wide):
    count, rows, columns = green_ref.shape
    offset_count = offset_ref.shape[0]
    none = jnp.zeros((REACH, rows, columns), jnp.float32)
    padded[:REACH] = none
    padded[REACH + count :] = none
    for e in range(count):
        padded[REACH + e] = green_ref[place_in[e]].astype(jnp.float32)
    wide[...] = coulomb_ref[...].astype(jnp.float32)
    column_tiles = columns // 128

    def tile(t, carry):
        row = pl.ds(pl.multiple_of(8 * (t // column_tiles), 8), 8)
        column = pl.ds(pl.multiple_of(128 * (t % column_tiles), 128), 128)
        strength = wide[row, column]
        own = padded[REACH : REACH + count, row, column]
        total = jnp.zeros(own.shape, jnp.float32)
        screened = []
        for k in range(offset_count):
            later = padded[pl.ds(REACH + offset_ref[k], count), row, column]
            polarization = (4.0 / count) * jnp.sum(own * later, axis=0)
            screened.append(strength * (1.0 + polarization * strength) * (1.0 / offset_count))
        for k in range(offset_count):
            total = total + screened[k][None] * padded[pl.ds(REACH - offset_ref[k], count), row, column]
        total = total.astype(jnp.bfloat16)
        for e in range(count):
            out_ref[place_out[e], row, column] = total[e]
        return carry

    lax.fori_loop(0, (rows // 8) * column_tiles, tile, 0)


def convolved(received, coulomb, offsets, place_in, place_out):
    count, rows, columns = received.shape
    return call(
        functools.partial(energy_body, place_in, place_out),
        jax.ShapeDtypeStruct((count, rows, columns), jnp.bfloat16),
        [SM, VM, VM],
        [pltpu.VMEM((count + 2 * REACH, rows, columns), jnp.float32), pltpu.VMEM((rows, columns), jnp.float32)],
    )(offsets, received, coulomb)


def all_to_all(value, axes):
    return lax.all_to_all(value, axes, split_axis=0, concat_axis=0, tiled=True)


def whole_run(energies, hamiltonian, coupling, coulomb, offsets):
    c, ham, strength = coupling[0], hamiltonian[0], coulomb[0]
    n = c.shape[0]
    parts = lax.axis_size(ENERGY)
    rows, pairs = n // parts, parts // 2
    count = 2 * parts
    place, x, core = lax.axis_index(SLAB), lax.axis_index("x"), lax.axis_index("core")
    edge = jnp.stack([place < lax.axis_size(SLAB) - 1, place > 0]).astype(jnp.float32)
    at = jnp.stack([core, x]).astype(jnp.int32)
    inverse = (1.0 / energies).astype(jnp.bfloat16).astype(jnp.float32)
    half = lambda value: lax.dynamic_slice_in_dim(value, core * (n // 2), n // 2, 0)
    wide = lambda *dims: jax.ShapeDtypeStruct(dims, jnp.float32)
    thin = lambda *dims: jax.ShapeDtypeStruct(dims, jnp.bfloat16)
    natural = list(range(count))
    by_chip = [(e % WIDTH) * (count // WIDTH) + e // WIDTH for e in range(count)]

    def run(body, out_shape, in_specs, *operands, scratch=()):
        return call(body, out_shape, in_specs, scratch)(*operands)

    lower_mine = passed_along(half(c), 1)
    ham_half = half(ham)
    ham_up = passed_along(ham_half, -1)
    ham_down = passed_along(ham_half, 1)
    energy_pair = swapped(energies)
    own, load = run(own_body, (wide(n, n), thin(n, n)), [SM, SM, VM, VM], edge[:1], at, c, ham)
    lower_theirs = swapped(lower_mine)
    one, three = row_ring(load, 1), row_ring(load, -1)
    pair, pair_half, _, lower_turned = run(
        pair_body, (wide(n, n), thin(n // 2, n), thin(n, n), thin(n, n)), [SM, VM, VM, VM],
        at, own, lower_mine, lower_theirs,
    )
    pair_up, pair_down = passed_along(pair_half, -1), passed_along(pair_half, 1)
    two = row_ring(one, 1)
    mine = [ham_up, ham_down, pair_up, pair_down]
    theirs = [swapped(v) for v in mine[:2]] + [swapped(v) for v in mine[2:]]
    chunks, first, second = run(
        second_body, (thin(parts, 2, rows, n), thin(n, n), thin(n, n)), [SM] * 4 + [VM] * 12,
        energies, inverse, edge, at, ham, pair, c, lower_turned, *mine, *theirs,
        scratch=[pltpu.VMEM((4, n, n), jnp.bfloat16)],
    )
    first, second = flipped(first, 0), flipped(second, 1)
    received = all_to_all(chunks, ENERGY)

    everything, give, last = run(
        gather_body, (thin(WIDTH, n, n), thin(2, n, n), thin(n, n)), [SM] + [VM] * 4,
        at, load, one, two, three,
    )
    below_c = row_above(last, False)
    got = swapped(give)
    outer_ham, inner_ham, far, mid, mid_turned, near = run(
        link_body, (thin(n, n),) * 6, [SM] + [VM] * 3, at, everything, got, below_c
    )
    outer, inner = run(role_body, (thin(n, n),) * 2, [SM, VM, VM], at, first, second)
    beyond = row_above(outer, True)
    beside = swapped(inner)
    open_outer, open_inner = run(
        open_body, (wide(n, n),) * 2, [SM] * 3 + [VM] * 10,
        at, energies, energy_pair, outer_ham, inner_ham, far, mid, mid_turned, near, outer, inner, beyond, beside,
    )
    result = convolved(received.reshape(count, rows, n), strength, offsets, natural, by_chip)
    self_mine = all_to_all(result, ("x", "zlo", "y")).reshape(WIDTH, pairs, rows, n)
    self_theirs = swapped(lax.dynamic_slice_in_dim(self_mine, 2 * (1 - core), 2, 0))
    mix = [pltpu.VMEM((pairs, 2, rows, n), jnp.bfloat16)]
    third = lambda role, opened, green: run(
        functools.partial(third_body, role), thin(n, n), [SM] + [VM] * 4,
        at, opened, self_mine, self_theirs, green, scratch=mix,
    )
    outer = third(False, open_outer, outer)
    beyond = row_above(outer, True)
    inner = third(True, open_inner, inner)
    beside = swapped(inner)
    open_outer, whole_inner, keep_inner, give_inner = run(
        inner_body, (wide(n, n), thin(n, n), thin(pairs, rows, n), thin(pairs, rows, n)),
        [SM] * 3 + [VM] * 10, at, energies, energy_pair, outer_ham, inner_ham, mid, mid_turned, near, self_mine,
        self_theirs, outer, inner, beside, scratch=mix,
    )
    got_inner = swapped(give_inner)
    whole_outer, chunks, give_outer = run(
        outer_body, (thin(n, n), thin(WIDTH, pairs, rows, n), thin(pairs, rows, n)), [SM] + [VM] * 6,
        at, far, open_outer, outer, beyond, keep_inner, got_inner, scratch=mix,
    )
    got_outer = swapped(give_outer)
    chunks = lax.dynamic_update_slice_in_dim(chunks, got_outer[None], 3 - 3 * core, 0)
    received = all_to_all(chunks.reshape(count, rows, n), ("x", "zlo", "y"))
    first, second = run(role_body, (thin(n, n),) * 2, [SM, VM, VM], at, whole_outer, whole_inner)
    first, second = flipped(first, 0), flipped(second, 1)
    result = convolved(received, strength, offsets, by_chip, natural)
    self_part = all_to_all(result.reshape(parts, 2, rows, n), ENERGY)
    green = run(spread_body, wide(2, n, n), [SM, VM, VM], at, first, second)
    self_part = jnp.swapaxes(self_part, 0, 1).reshape(2, n, n)
    return (green[:, None], self_part[:, None])


def fine_mesh(mesh):
    energy, slab = mesh.shape["energy"], mesh.shape["slab"]
    zlo, y = (2, energy // 4) if energy > 2 else (1, 1)
    devices = mesh.devices.reshape(zlo, y, 2, slab // WIDTH, WIDTH)
    return jax.sharding.Mesh(devices, ("zlo", "y", "core", "row", "x"))


def solution(mesh):
    mesh = fine_mesh(mesh)
    return jax.shard_map(
        whole_run,
        mesh=mesh,
        in_specs=(P(ENERGY), P(SLAB), P(SLAB), P(SLAB, ENERGY), P()),
        out_specs=(P(ENERGY, SLAB), P(ENERGY, SLAB)),
        check_vma=False,
    )
```

```python
import functools

import jax
import jax.numpy as jnp
from jax import lax
from jax.experimental import pallas as pl
from jax.experimental.pallas import tpu as pltpu
from jax.sharding import PartitionSpec as P


BROAD = 0.3
REACH = 16

VM = pl.BlockSpec(memory_space=pltpu.VMEM)
SM = pl.BlockSpec(memory_space=pltpu.SMEM)


SLAB = ("row", "x")
ENERGY = ("zlo", "y", "core")
WIDTH = 4


def passed_along(value, steps):
    count = lax.axis_size(SLAB)
    leading, last = (max(0, -steps), min(count, count - steps))
    return lax.ppermute(value, SLAB, [(source, source + steps) for source in range(leading, last)])


def row_ring(value, steps):
    return lax.ppermute(value, "x", [(s, (s + steps) % WIDTH) for s in range(WIDTH)])


def swapped(value):
    return lax.ppermute(value, "core", [(0, 1), (1, 0)])


def row_above(value, both):
    rows = lax.axis_size("row")
    pairs = [(rows + r, r + 1) for r in range(rows - 1)]
    if both:
        pairs += [(r, rows + r - 1) for r in range(1, rows)]
    return lax.ppermute(value, ("core", "row"), pairs)


def flipped(value, side):
    pairs = [(c * WIDTH + i, (i // 2) * WIDTH + 2 * c + (i % 2 + side) % 2) for c in range(2) for i in range(WIDTH)]
    return lax.ppermute(value, ("core", "x"), pairs)


def call(body, out_shape, in_specs, scratch=()):
    return pl.pallas_call(
        body,
        out_shape=out_shape,
        in_specs=in_specs,
        out_specs=jax.tree.map(lambda _: VM, out_shape),
        scratch_shapes=list(scratch),
        compiler_params=pltpu.CompilerParams(vmem_limit_bytes=16 * 1024 * 1024),
    )


def dot(a, b):
    return jnp.dot(a, b, preferred_element_type=jnp.float32)


def dot_t(a, b):
    return lax.dot_general(a, b, (((1,), (1,)), ((), ())), preferred_element_type=jnp.float32)


def tables(n):
    row = lax.broadcasted_iota(jnp.int32, (n, n), 0)
    col = lax.broadcasted_iota(jnp.int32, (n, n), 1)
    half = n // 2
    eye = jnp.where(row == col, 1.0, 0.0)
    rotate = jnp.where(col == row + half, -1.0, 0.0) + jnp.where(col == row - half, 1.0, 0.0)
    return eye, rotate


def own_body(keep_ref, at_ref, c_ref, ham_ref, own_ref, load_ref):
    own_ref[...] = dot_t(c_ref[...], c_ref[...]) * keep_ref[0]
    load_ref[...] = jnp.where(at_ref[0] == 0, ham_ref[...], c_ref[...])


def returned(value, inner, slot):
    pairs = []
    for c in range(2):
        block = (1 + c) if inner else 3 * c
        pairs += [(c * WIDTH + i, (i // 2) * WIDTH + block) for i in range(slot, WIDTH, 2)]
    return lax.ppermute(value, ("core", "x"), pairs)


def place_halves(core, whole, mine, theirs):
    half = mine.shape[0]
    whole[pl.ds(pl.multiple_of(core * half, half), half)] = mine
    whole[pl.ds(pl.multiple_of((1 - core) * half, half), half)] = theirs


def pair_body(at_ref, own_ref, mine_ref, theirs_ref, pair_ref, half_ref, below_ref, turned_ref):
    core = at_ref[0]
    half = half_ref.shape[0]
    place_halves(core, below_ref, mine_ref[...], theirs_ref[...])
    below = below_ref[...]
    turned = below.T
    turned_ref[...] = turned
    pair_ref[...] = own_ref[...] + dot(turned, below)
    half_ref[...] = pair_ref[pl.ds(pl.multiple_of(core * half, half), half)].astype(jnp.bfloat16)


def first_step(energy, inverse, ham, pair, eye):
    square = inverse * inverse
    return (
        (square * inverse) * pair.astype(jnp.float32) + square * ham + (2.0 * inverse - square * energy) * eye
    ).astype(jnp.bfloat16)


def linked(green, link):
    return dot(link, dot_t(green, link).astype(jnp.bfloat16))


def finish(matrix, green, eye):
    product = dot(matrix, green)
    residue = (2.0 * eye - product).astype(jnp.bfloat16)
    return dot(green, residue)


def second_body(
    energy_ref, inverse_ref, edge_ref, at_ref, ham_ref, pair_ref, c_ref, lower_turned_ref, *refs
):
    mine_refs, theirs_refs = refs[:4], refs[4:8]
    out_ref, first_ref, second_ref, whole = refs[8:]
    n = c_ref.shape[0]
    eye, rotate = tables(n)
    chunks = out_ref.shape[0]
    for i in range(4):
        place_halves(at_ref[0], whole.at[i], mine_refs[i][...], theirs_refs[i][...])
    odd = lax.rem(at_ref[1], 2)
    turn = BROAD * rotate
    ham = ham_ref[...].astype(jnp.float32) - turn
    ham_above = whole[0].astype(jnp.float32) - turn
    ham_below = whole[1].astype(jnp.float32) - turn
    for e, same_ref in ((odd, first_ref), (1 - odd, second_ref)):
        energy, inverse = energy_ref[e], inverse_ref[e]
        above = first_step(energy, inverse * edge_ref[0], ham_above, whole[2], eye)
        below = first_step(energy, inverse * edge_ref[1], ham_below, whole[3], eye)
        green = first_step(energy, inverse, ham, pair_ref[...], eye)
        terms = linked(above, c_ref[...]) + linked(below, lower_turned_ref[...])
        matrix = (energy * eye - ham - terms).astype(jnp.bfloat16)
        result = finish(matrix, green, eye).astype(jnp.bfloat16)
        out_ref[:, e] = result.reshape(chunks, n // chunks, n)
        same_ref[...] = result


def gather_body(at_ref, here_ref, one_ref, two_ref, three_ref, all_ref, give_ref, last_ref):
    core, x = at_ref[0], at_ref[1]
    for k, ref in enumerate((here_ref, one_ref, two_ref, three_ref)):
        all_ref[lax.rem(x + WIDTH - k, WIDTH)] = ref[...]
    give_ref[...] = all_ref[pl.ds(2 * (1 - core), 2)]
    last_ref[...] = all_ref[WIDTH - 1]


def link_body(at_ref, all_ref, got_ref, below_ref, outer_ham, inner_ham, far, mid, mid_turned, near):
    @pl.when(at_ref[0] == 0)
    def _():
        outer_ham[...] = all_ref[0]
        inner_ham[...] = all_ref[1]
        far[...] = below_ref[...].T
        mid[...] = got_ref[0]
        mid_turned[...] = got_ref[0].T
        near[...] = got_ref[1]

    @pl.when(at_ref[0] == 1)
    def _():
        outer_ham[...] = got_ref[1]
        inner_ham[...] = got_ref[0]
        far[...] = all_ref[3]
        mid[...] = all_ref[2].T
        mid_turned[...] = all_ref[2]
        near[...] = all_ref[1].T


def row_energy(at_ref, energy_ref, pair_ref):
    core, x = at_ref[0], at_ref[1]
    return jnp.where(x // 2 == core, energy_ref[lax.rem(x, 2)], pair_ref[lax.rem(x, 2)])


def role_body(at_ref, first_ref, second_ref, outer_ref, inner_ref):
    match = lax.rem(at_ref[1], 2) == at_ref[0]
    outer_ref[...] = jnp.where(match, first_ref[...], second_ref[...])
    inner_ref[...] = jnp.where(match, second_ref[...], first_ref[...])


def open_body(
    at_ref, energy_ref, energy_pair_ref, outer_ham, inner_ham, far, mid, mid_turned, near, outer, inner, beyond, beside, open_outer, open_inner,
):
    eye, rotate = tables(outer.shape[0])
    base = row_energy(at_ref, energy_ref, energy_pair_ref) * eye + BROAD * rotate
    open_outer[...] = (
        base - outer_ham[...].astype(jnp.float32) - linked(inner[...], mid[...]) - linked(beyond[...], far[...])
    )
    open_inner[...] = (
        base - inner_ham[...].astype(jnp.float32) - linked(outer[...], mid_turned[...]) - linked(beside[...], near[...])
    )


def joined_rows(core, slot, mine_ref, theirs_ref, scratch):
    scratch[:, core] = mine_ref[2 * core + slot]
    scratch[:, 1 - core] = theirs_ref[slot]
    n = scratch.shape[-1]
    return scratch[...].reshape(n, n).astype(jnp.float32)


def third_body(inner, at_ref, open_ref, mine_ref, theirs_ref, green_ref, out_ref, scratch):
    core = at_ref[0]
    eye, _ = tables(open_ref.shape[0])
    self_part = joined_rows(core, 1 - core if inner else core, mine_ref, theirs_ref, scratch)
    matrix = (open_ref[...] - self_part).astype(jnp.bfloat16)
    out_ref[...] = finish(matrix, green_ref[...], eye).astype(jnp.bfloat16)


def split_rows(core, result, keep_ref, give_ref, scratch):
    scratch[...] = result.reshape(scratch.shape)
    keep_ref[...] = scratch[:, core]
    give_ref[...] = scratch[:, 1 - core]


def part_body(
    at_ref, energy_ref, energy_pair_ref, outer_ham, inner_ham, mid, mid_turned, mine_ref, theirs_ref, outer, inner,
    open_outer, open_inner, scratch,
):
    core = at_ref[0]
    eye, rotate = tables(outer.shape[0])
    base = row_energy(at_ref, energy_ref, energy_pair_ref) * eye + BROAD * rotate
    self_part = joined_rows(core, 1 - core, mine_ref, theirs_ref, scratch)
    open_inner[...] = base - inner_ham[...].astype(jnp.float32) - self_part - linked(outer[...], mid_turned[...])
    self_part = joined_rows(core, core, mine_ref, theirs_ref, scratch)
    open_outer[...] = base - outer_ham[...].astype(jnp.float32) - self_part - linked(inner[...], mid[...])


def inner_body(at_ref, near, open_ref, inner, beside, whole_ref, keep_ref, give_ref, scratch):
    eye, _ = tables(inner.shape[0])
    matrix = (open_ref[...] - linked(beside[...], near[...])).astype(jnp.bfloat16)
    result = finish(matrix, inner[...], eye).astype(jnp.bfloat16)
    whole_ref[...] = result
    split_rows(at_ref[0], result, keep_ref, give_ref, scratch)


def outer_body(
    at_ref, far, open_ref, outer, beyond, keep_inner, got_inner, whole_ref, out_ref, give_ref, scratch
):
    core = at_ref[0]
    eye, _ = tables(outer.shape[0])
    matrix = (open_ref[...] - linked(beyond[...], far[...])).astype(jnp.bfloat16)
    result = finish(matrix, outer[...], eye).astype(jnp.bfloat16)
    whole_ref[...] = result
    scratch[...] = result.reshape(scratch.shape)
    give_ref[...] = scratch[:, 1 - core]
    out_ref[3 * core] = scratch[:, core]
    out_ref[1 + core] = keep_inner[...]
    out_ref[2 - core] = got_inner[...]
    out_ref[3 - 3 * core] = got_inner[...]


def spread_body(at_ref, inner_0, inner_1, outer_0, outer_1, out_ref):
    within = jnp.logical_and(at_ref[1] > 0, at_ref[1] < WIDTH - 1)
    out_ref[0] = jnp.where(within, inner_0[...], outer_0[...]).astype(jnp.float32)
    out_ref[1] = jnp.where(within, inner_1[...], outer_1[...]).astype(jnp.float32)


def energy_body(place_in, place_out, offset_ref, green_ref, coulomb_ref, out_ref, padded):
    count, rows, columns = green_ref.shape
    offset_count = offset_ref.shape[0]
    none = jnp.zeros((REACH, 8, 128), jnp.float32)
    padded[:REACH] = none
    padded[REACH + count :] = none
    column_tiles = columns // 128

    def tile(t, carry):
        row = pl.ds(pl.multiple_of(8 * (t // column_tiles), 8), 8)
        column = pl.ds(pl.multiple_of(128 * (t % column_tiles), 128), 128)
        strength = coulomb_ref[row, column].astype(jnp.float32)
        own = [green_ref[place_in[e], row, column].astype(jnp.float32) for e in range(count)]
        for e in range(count):
            padded[REACH + e] = own[e]
        screened = []
        for k in range(offset_count):
            later = padded.at[pl.ds(REACH + offset_ref[k], count)]
            sums = [own[e] * later[e] for e in range(4)]
            for e in range(4, count):
                sums[e % 4] = sums[e % 4] + own[e] * later[e]
            polarization = (4.0 / count) * ((sums[0] + sums[1]) + (sums[2] + sums[3]))
            screened.append(strength * (1.0 + polarization * strength) * (1.0 / offset_count))
        earlier = [padded.at[pl.ds(REACH - offset_ref[k], count)] for k in range(offset_count)]
        for e in range(count):
            terms = [screened[k] * earlier[k][e] for k in range(offset_count)]
            while len(terms) > 1:
                terms = [a + b for a, b in zip(terms[::2], terms[1::2])] + terms[len(terms) // 2 * 2 :]
            out_ref[place_out[e], row, column] = terms[0].astype(jnp.bfloat16)
        return carry

    lax.fori_loop(0, (rows // 8) * column_tiles, tile, 0)


def convolved(received, coulomb, offsets, place_in, place_out):
    count, rows, columns = received.shape
    return call(
        functools.partial(energy_body, place_in, place_out),
        jax.ShapeDtypeStruct((count, rows, columns), jnp.bfloat16),
        [SM, VM, VM],
        [pltpu.VMEM((count + 2 * REACH, 8, 128), jnp.float32)],
    )(offsets, received, coulomb)


def all_to_all(value, axes):
    return lax.all_to_all(value, axes, split_axis=0, concat_axis=0, tiled=True)


def whole_run(energies, hamiltonian, coupling, coulomb, offsets):
    c, ham, strength = coupling[0], hamiltonian[0], coulomb[0]
    n = c.shape[0]
    parts = lax.axis_size(ENERGY)
    rows, pairs = n // parts, parts // 2
    count = 2 * parts
    place, x, core = lax.axis_index(SLAB), lax.axis_index("x"), lax.axis_index("core")
    edge = jnp.stack([place < lax.axis_size(SLAB) - 1, place > 0]).astype(jnp.float32)
    at = jnp.stack([core, x]).astype(jnp.int32)
    inverse = (1.0 / energies).astype(jnp.bfloat16).astype(jnp.float32)
    half = lambda value: lax.dynamic_slice_in_dim(value, core * (n // 2), n // 2, 0)
    wide = lambda *dims: jax.ShapeDtypeStruct(dims, jnp.float32)
    thin = lambda *dims: jax.ShapeDtypeStruct(dims, jnp.bfloat16)
    natural = list(range(count))
    by_chip = [(e % WIDTH) * (count // WIDTH) + e // WIDTH for e in range(count)]

    def run(body, out_shape, in_specs, *operands, scratch=()):
        return call(body, out_shape, in_specs, scratch)(*operands)

    lower_mine = passed_along(half(c), 1)
    ham_half = half(ham)
    ham_up = passed_along(ham_half, -1)
    ham_down = passed_along(ham_half, 1)
    energy_pair = swapped(energies)
    own, load = run(own_body, (wide(n, n), thin(n, n)), [SM, SM, VM, VM], edge[:1], at, c, ham)
    lower_theirs = swapped(lower_mine)
    one, three = row_ring(load, 1), row_ring(load, -1)
    pair, pair_half, _, lower_turned = run(
        pair_body, (wide(n, n), thin(n // 2, n), thin(n, n), thin(n, n)), [SM, VM, VM, VM],
        at, own, lower_mine, lower_theirs,
    )
    pair_up, pair_down = passed_along(pair_half, -1), passed_along(pair_half, 1)
    two = row_ring(one, 1)
    mine = [ham_up, ham_down, pair_up, pair_down]
    theirs = [swapped(v) for v in mine[:2]] + [swapped(v) for v in mine[2:]]
    chunks, first, second = run(
        second_body, (thin(parts, 2, rows, n), thin(n, n), thin(n, n)), [SM] * 4 + [VM] * 12,
        energies, inverse, edge, at, ham, pair, c, lower_turned, *mine, *theirs,
        scratch=[pltpu.VMEM((4, n, n), jnp.bfloat16)],
    )
    first, second = flipped(first, 0), flipped(second, 1)
    received = all_to_all(chunks, ENERGY)

    everything, give, last = run(
        gather_body, (thin(WIDTH, n, n), thin(2, n, n), thin(n, n)), [SM] + [VM] * 4,
        at, load, one, two, three,
    )
    below_c = row_above(last, False)
    got = swapped(give)
    outer_ham, inner_ham, far, mid, mid_turned, near = run(
        link_body, (thin(n, n),) * 6, [SM] + [VM] * 3, at, everything, got, below_c
    )
    outer, inner = run(role_body, (thin(n, n),) * 2, [SM, VM, VM], at, first, second)
    beyond = row_above(outer, True)
    beside = swapped(inner)
    open_outer, open_inner = run(
        open_body, (wide(n, n),) * 2, [SM] * 3 + [VM] * 10,
        at, energies, energy_pair, outer_ham, inner_ham, far, mid, mid_turned, near, outer, inner, beyond, beside,
    )
    result = convolved(received.reshape(count, rows, n), strength, offsets, natural, by_chip)
    self_mine = all_to_all(result, ("x", "zlo", "y")).reshape(WIDTH, pairs, rows, n)
    self_theirs = swapped(lax.dynamic_slice_in_dim(self_mine, 2 * (1 - core), 2, 0))
    mix = [pltpu.VMEM((pairs, 2, rows, n), jnp.bfloat16)]
    third = lambda role, opened, green: run(
        functools.partial(third_body, role), thin(n, n), [SM] + [VM] * 4,
        at, opened, self_mine, self_theirs, green, scratch=mix,
    )
    outer = third(False, open_outer, outer)
    beyond = row_above(outer, True)
    inner = third(True, open_inner, inner)
    beside = swapped(inner)
    open_outer, open_inner = run(
        part_body, (wide(n, n), wide(n, n)), [SM] * 3 + [VM] * 8, at, energies, energy_pair,
        outer_ham, inner_ham, mid, mid_turned, self_mine, self_theirs, outer, inner, scratch=mix,
    )
    whole_inner, keep_inner, give_inner = run(
        inner_body, (thin(n, n), thin(pairs, rows, n), thin(pairs, rows, n)), [SM] + [VM] * 4,
        at, near, open_inner, inner, beside, scratch=mix,
    )
    back_inner = [returned(whole_inner, True, slot) for slot in range(2)]
    got_inner = swapped(give_inner)
    whole_outer, chunks, give_outer = run(
        outer_body, (thin(n, n), thin(WIDTH, pairs, rows, n), thin(pairs, rows, n)), [SM] + [VM] * 6,
        at, far, open_outer, outer, beyond, keep_inner, got_inner, scratch=mix,
    )
    got_outer = swapped(give_outer)
    chunks = lax.dynamic_update_slice_in_dim(chunks, got_outer[None], 3 - 3 * core, 0)
    received = all_to_all(chunks.reshape(count, rows, n), ("x", "zlo", "y"))
    back_outer = [returned(whole_outer, False, slot) for slot in range(2)]
    result = convolved(received, strength, offsets, by_chip, natural)
    self_part = all_to_all(result.reshape(parts, 2, rows, n), ENERGY)
    green = run(spread_body, wide(2, n, n), [SM] + [VM] * 4, at, *back_inner, *back_outer)
    self_part = jnp.swapaxes(self_part, 0, 1).reshape(2, n, n)
    return (green[:, None], self_part[:, None])


def fine_mesh(mesh):
    energy, slab = mesh.shape["energy"], mesh.shape["slab"]
    zlo, y = (2, energy // 4) if energy > 2 else (1, 1)
    devices = mesh.devices.reshape(zlo, y, 2, slab // WIDTH, WIDTH)
    return jax.sharding.Mesh(devices, ("zlo", "y", "core", "row", "x"))


def solution(mesh):
    mesh = fine_mesh(mesh)
    return jax.shard_map(
        whole_run,
        mesh=mesh,
        in_specs=(P(ENERGY), P(SLAB), P(SLAB), P(SLAB, ENERGY), P()),
        out_specs=(P(ENERGY, SLAB), P(ENERGY, SLAB)),
        check_vma=False,
    )
```

```python
import functools

import jax
import jax.numpy as jnp
from jax import lax
from jax.experimental import pallas as pl
from jax.experimental.pallas import tpu as pltpu
from jax.sharding import PartitionSpec as P


BROAD = 0.3
REACH = 16

VM = pl.BlockSpec(memory_space=pltpu.VMEM)
SM = pl.BlockSpec(memory_space=pltpu.SMEM)


SLAB = ("row", "x")
ENERGY = ("zlo", "y", "core")
WIDTH = 4


def passed_along(value, steps):
    count = lax.axis_size(SLAB)
    leading, last = (max(0, -steps), min(count, count - steps))
    return lax.ppermute(value, SLAB, [(source, source + steps) for source in range(leading, last)])


def row_ring(value, steps):
    return lax.ppermute(value, "x", [(s, (s + steps) % WIDTH) for s in range(WIDTH)])


def swapped(value):
    return lax.ppermute(value, "core", [(0, 1), (1, 0)])


def row_above(value):
    rows = lax.axis_size("row")
    pairs = [(rows + r, r + 1) for r in range(rows - 1)] + [(r, rows + r - 1) for r in range(1, rows)]
    return lax.ppermute(value, ("core", "row"), pairs)


def climbed(value):
    rows = lax.axis_size("row")
    pairs = [(r * WIDTH, (r + 1) * WIDTH) for r in range(rows - 1)]
    pairs += [(r * WIDTH + WIDTH - 1, r * WIDTH - 1) for r in range(1, rows)]
    return lax.ppermute(value, ("core", "row", "x"), pairs)


def sent(value, pairs):
    return lax.ppermute(value, ("core", "x"), [(a * WIDTH + i, b * WIDTH + j) for (a, i), (b, j) in pairs])


def flipped(value, side):
    pairs = [(c * WIDTH + i, (i // 2) * WIDTH + 2 * c + (i % 2 + side) % 2) for c in range(2) for i in range(WIDTH)]
    return lax.ppermute(value, ("core", "x"), pairs)


def call(body, out_shape, in_specs, scratch=()):
    return pl.pallas_call(
        body,
        out_shape=out_shape,
        in_specs=in_specs,
        out_specs=jax.tree.map(lambda _: VM, out_shape),
        scratch_shapes=list(scratch),
        compiler_params=pltpu.CompilerParams(vmem_limit_bytes=16 * 1024 * 1024),
    )


def dot(a, b):
    return jnp.dot(a, b, preferred_element_type=jnp.float32)


def dot_t(a, b):
    return lax.dot_general(a, b, (((1,), (1,)), ((), ())), preferred_element_type=jnp.float32)


def tables(n):
    row = lax.broadcasted_iota(jnp.int32, (n, n), 0)
    col = lax.broadcasted_iota(jnp.int32, (n, n), 1)
    half = n // 2
    eye = jnp.where(row == col, 1.0, 0.0)
    rotate = jnp.where(col == row + half, -1.0, 0.0) + jnp.where(col == row - half, 1.0, 0.0)
    return eye, rotate


def own_body(keep_ref, at_ref, c_ref, ham_ref, own_ref, load_ref):
    own_ref[...] = dot_t(c_ref[...], c_ref[...]) * keep_ref[0]
    load_ref[...] = jnp.where(at_ref[0] == 0, ham_ref[...], c_ref[...])


def returned(value, inner, slot):
    pairs = []
    for c in range(2):
        block = (1 + c) if inner else 3 * c
        pairs += [(c * WIDTH + i, (i // 2) * WIDTH + block) for i in range(slot, WIDTH, 2)]
    return lax.ppermute(value, ("core", "x"), pairs)


def place_halves(core, whole, mine, theirs):
    half = mine.shape[0]
    whole[pl.ds(pl.multiple_of(core * half, half), half)] = mine
    whole[pl.ds(pl.multiple_of((1 - core) * half, half), half)] = theirs


def pair_body(at_ref, own_ref, mine_ref, theirs_ref, pair_ref, half_ref, below_ref, turned_ref):
    core = at_ref[0]
    half = half_ref.shape[0]
    place_halves(core, below_ref, mine_ref[...], theirs_ref[...])
    below = below_ref[...]
    turned = below.T
    turned_ref[...] = turned
    pair_ref[...] = own_ref[...] + dot(turned, below)
    half_ref[...] = pair_ref[pl.ds(pl.multiple_of(core * half, half), half)].astype(jnp.bfloat16)


def first_step(energy, inverse, ham, pair, eye):
    square = inverse * inverse
    return (
        (square * inverse) * pair.astype(jnp.float32) + square * ham + (2.0 * inverse - square * energy) * eye
    ).astype(jnp.bfloat16)


def linked(green, link):
    return dot(link, dot_t(green, link).astype(jnp.bfloat16))


def finish(matrix, green, eye):
    product = dot(matrix, green)
    residue = (2.0 * eye - product).astype(jnp.bfloat16)
    return dot(green, residue)


def near_body(at_ref, one_ref, three_ref, climbed_ref, previous_ref, next_ref):
    first = at_ref[0] == 0
    previous_ref[...] = jnp.where(jnp.logical_and(first, at_ref[1] == 0), climbed_ref[...], one_ref[...])
    next_ref[...] = jnp.where(jnp.logical_and(first, at_ref[1] == WIDTH - 1), climbed_ref[...], three_ref[...])


def second_body(
    energy_ref, inverse_ref, edge_ref, at_ref, ham_ref, pair_ref, c_ref, lower_turned_ref, previous_ref, next_ref,
    got_previous_ref, got_next_ref, up_ref, down_ref, got_up_ref, got_down_ref, out_ref, first_ref, second_ref, whole,
):
    n = c_ref.shape[0]
    eye, rotate = tables(n)
    chunks = out_ref.shape[0]
    first = at_ref[0] == 0
    whole[0] = jnp.where(first, next_ref[...], got_next_ref[...])
    whole[1] = jnp.where(first, previous_ref[...], got_previous_ref[...])
    place_halves(at_ref[0], whole.at[2], up_ref[...], got_up_ref[...])
    place_halves(at_ref[0], whole.at[3], down_ref[...], got_down_ref[...])
    odd = lax.rem(at_ref[1], 2)
    turn = BROAD * rotate
    ham = ham_ref[...].astype(jnp.float32) - turn
    ham_above = whole[0].astype(jnp.float32) - turn
    ham_below = whole[1].astype(jnp.float32) - turn
    for e, same_ref in ((odd, first_ref), (1 - odd, second_ref)):
        energy, inverse = energy_ref[e], inverse_ref[e]
        above = first_step(energy, inverse * edge_ref[0], ham_above, whole[2], eye)
        below = first_step(energy, inverse * edge_ref[1], ham_below, whole[3], eye)
        green = first_step(energy, inverse, ham, pair_ref[...], eye)
        terms = linked(above, c_ref[...]) + linked(below, lower_turned_ref[...])
        matrix = (energy * eye - ham - terms).astype(jnp.bfloat16)
        result = finish(matrix, green, eye).astype(jnp.bfloat16)
        out_ref[:, e] = result.reshape(chunks, n // chunks, n)
        same_ref[...] = result


def link_body(
    at_ref, c_ref, ham_ref, below_ref, near_ref, middle_ref, mine_1, mine_2, mine_3, other_1, other_2, other_3, extra,
    outer_ham, inner_ham, far, mid, mid_turned, near,
):
    x = at_ref[1]

    def block(b, here, one, two, three):
        k = lax.rem(x + WIDTH - b, WIDTH)
        return jnp.where(k == 0, here, jnp.where(k == 1, one, jnp.where(k == 2, two, three)))

    @pl.when(at_ref[0] == 0)
    def _():
        hams = (ham_ref[...], mine_1[...], mine_2[...], mine_3[...])
        links = (c_ref[...], other_1[...], other_2[...], other_3[...])
        outer_ham[...] = block(0, *hams)
        inner_ham[...] = block(1, *hams)
        far[...] = jnp.where(x == 0, below_ref[...], jnp.where(x == 2, middle_ref[...], near_ref[...])).T
        middle = block(0, *links)
        mid[...] = middle
        mid_turned[...] = middle.T
        near[...] = block(1, *links)

    @pl.when(at_ref[0] == 1)
    def _():
        hams = (ham_ref[...], jnp.where(x == 0, extra[...], other_1[...]), other_2[...], other_3[...])
        links = (c_ref[...], mine_1[...], mine_2[...], mine_3[...])
        outer_ham[...] = block(3, *hams)
        inner_ham[...] = block(2, *hams)
        far[...] = block(3, *links)
        middle = block(2, *links)
        mid[...] = middle.T
        mid_turned[...] = middle
        near[...] = block(1, *links).T


def row_energy(at_ref, energy_ref, pair_ref):
    core, x = at_ref[0], at_ref[1]
    return jnp.where(x // 2 == core, energy_ref[lax.rem(x, 2)], pair_ref[lax.rem(x, 2)])


def role_body(at_ref, first_ref, second_ref, outer_ref, inner_ref):
    match = lax.rem(at_ref[1], 2) == at_ref[0]
    outer_ref[...] = jnp.where(match, first_ref[...], second_ref[...])
    inner_ref[...] = jnp.where(match, second_ref[...], first_ref[...])


def open_body(
    at_ref, energy_ref, energy_pair_ref, outer_ham, inner_ham, far, mid, mid_turned, near, outer, inner, beyond, beside, open_outer, open_inner,
):
    eye, rotate = tables(outer.shape[0])
    base = row_energy(at_ref, energy_ref, energy_pair_ref) * eye + BROAD * rotate
    open_outer[...] = (
        base - outer_ham[...].astype(jnp.float32) - linked(inner[...], mid[...]) - linked(beyond[...], far[...])
    )
    open_inner[...] = (
        base - inner_ham[...].astype(jnp.float32) - linked(outer[...], mid_turned[...]) - linked(beside[...], near[...])
    )


def joined_rows(core, slot, mine_ref, theirs_ref, scratch):
    scratch[:, core] = mine_ref[2 * core + slot]
    scratch[:, 1 - core] = theirs_ref[slot]
    n = scratch.shape[-1]
    return scratch[...].reshape(n, n).astype(jnp.float32)


def third_body(inner, at_ref, open_ref, mine_ref, theirs_ref, green_ref, out_ref, scratch):
    core = at_ref[0]
    eye, _ = tables(open_ref.shape[0])
    self_part = joined_rows(core, 1 - core if inner else core, mine_ref, theirs_ref, scratch)
    matrix = (open_ref[...] - self_part).astype(jnp.bfloat16)
    out_ref[...] = finish(matrix, green_ref[...], eye).astype(jnp.bfloat16)


def split_rows(core, result, keep_ref, give_ref, scratch):
    scratch[...] = result.reshape(scratch.shape)
    keep_ref[...] = scratch[:, core]
    give_ref[...] = scratch[:, 1 - core]


def part_body(
    at_ref, energy_ref, energy_pair_ref, outer_ham, inner_ham, mid, mid_turned, mine_ref, theirs_ref, outer, inner,
    open_outer, open_inner, scratch,
):
    core = at_ref[0]
    eye, rotate = tables(outer.shape[0])
    base = row_energy(at_ref, energy_ref, energy_pair_ref) * eye + BROAD * rotate
    self_part = joined_rows(core, 1 - core, mine_ref, theirs_ref, scratch)
    open_inner[...] = base - inner_ham[...].astype(jnp.float32) - self_part - linked(outer[...], mid_turned[...])
    self_part = joined_rows(core, core, mine_ref, theirs_ref, scratch)
    open_outer[...] = base - outer_ham[...].astype(jnp.float32) - self_part - linked(inner[...], mid[...])


def inner_body(at_ref, near, open_ref, inner, beside, whole_ref, keep_ref, give_ref, scratch):
    eye, _ = tables(inner.shape[0])
    matrix = (open_ref[...] - linked(beside[...], near[...])).astype(jnp.bfloat16)
    result = finish(matrix, inner[...], eye).astype(jnp.bfloat16)
    whole_ref[...] = result
    split_rows(at_ref[0], result, keep_ref, give_ref, scratch)


def outer_body(
    at_ref, far, open_ref, outer, beyond, keep_inner, got_inner, whole_ref, out_ref, give_ref, scratch
):
    core = at_ref[0]
    eye, _ = tables(outer.shape[0])
    matrix = (open_ref[...] - linked(beyond[...], far[...])).astype(jnp.bfloat16)
    result = finish(matrix, outer[...], eye).astype(jnp.bfloat16)
    whole_ref[...] = result
    scratch[...] = result.reshape(scratch.shape)
    give_ref[...] = scratch[:, 1 - core]
    out_ref[3 * core] = scratch[:, core]
    out_ref[1 + core] = keep_inner[...]
    out_ref[2 - core] = got_inner[...]
    out_ref[3 - 3 * core] = got_inner[...]


def spread_body(at_ref, inner_0, inner_1, outer_0, outer_1, out_ref):
    within = jnp.logical_and(at_ref[1] > 0, at_ref[1] < WIDTH - 1)
    out_ref[0] = jnp.where(within, inner_0[...], outer_0[...]).astype(jnp.float32)
    out_ref[1] = jnp.where(within, inner_1[...], outer_1[...]).astype(jnp.float32)


def energy_body(place_in, place_out, offset_ref, green_ref, coulomb_ref, out_ref, padded):
    count, rows, columns = green_ref.shape
    offset_count = offset_ref.shape[0]
    none = jnp.zeros((REACH, 8, 128), jnp.float32)
    padded[:REACH] = none
    padded[REACH + count :] = none
    column_tiles = columns // 128

    def tile(t, carry):
        row = pl.ds(pl.multiple_of(8 * (t // column_tiles), 8), 8)
        column = pl.ds(pl.multiple_of(128 * (t % column_tiles), 128), 128)
        strength = coulomb_ref[row, column].astype(jnp.float32)
        own = [green_ref[place_in[e], row, column].astype(jnp.float32) for e in range(count)]
        for e in range(count):
            padded[REACH + e] = own[e]
        screened = []
        for k in range(offset_count):
            later = padded.at[pl.ds(REACH + offset_ref[k], count)]
            sums = [own[e] * later[e] for e in range(4)]
            for e in range(4, count):
                sums[e % 4] = sums[e % 4] + own[e] * later[e]
            polarization = (4.0 / count) * ((sums[0] + sums[1]) + (sums[2] + sums[3]))
            screened.append(strength * (1.0 + polarization * strength) * (1.0 / offset_count))
        earlier = [padded.at[pl.ds(REACH - offset_ref[k], count)] for k in range(offset_count)]
        for e in range(count):
            terms = [screened[k] * earlier[k][e] for k in range(offset_count)]
            while len(terms) > 1:
                terms = [a + b for a, b in zip(terms[::2], terms[1::2])] + terms[len(terms) // 2 * 2 :]
            out_ref[place_out[e], row, column] = terms[0].astype(jnp.bfloat16)
        return carry

    lax.fori_loop(0, (rows // 8) * column_tiles, tile, 0)


def convolved(received, coulomb, offsets, place_in, place_out):
    count, rows, columns = received.shape
    return call(
        functools.partial(energy_body, place_in, place_out),
        jax.ShapeDtypeStruct((count, rows, columns), jnp.bfloat16),
        [SM, VM, VM],
        [pltpu.VMEM((count + 2 * REACH, 8, 128), jnp.float32)],
    )(offsets, received, coulomb)


def all_to_all(value, axes):
    return lax.all_to_all(value, axes, split_axis=0, concat_axis=0, tiled=True)


def whole_run(energies, hamiltonian, coupling, coulomb, offsets):
    c, ham, strength = coupling[0], hamiltonian[0], coulomb[0]
    n = c.shape[0]
    parts = lax.axis_size(ENERGY)
    rows, pairs = n // parts, parts // 2
    count = 2 * parts
    place, x, core = lax.axis_index(SLAB), lax.axis_index("x"), lax.axis_index("core")
    edge = jnp.stack([place < lax.axis_size(SLAB) - 1, place > 0]).astype(jnp.float32)
    at = jnp.stack([core, x]).astype(jnp.int32)
    inverse = (1.0 / energies).astype(jnp.bfloat16).astype(jnp.float32)
    half = lambda value: lax.dynamic_slice_in_dim(value, core * (n // 2), n // 2, 0)
    wide = lambda *dims: jax.ShapeDtypeStruct(dims, jnp.float32)
    thin = lambda *dims: jax.ShapeDtypeStruct(dims, jnp.bfloat16)
    natural = list(range(count))
    by_chip = [(e % WIDTH) * (count // WIDTH) + e // WIDTH for e in range(count)]

    def run(body, out_shape, in_specs, *operands, scratch=()):
        return call(body, out_shape, in_specs, scratch)(*operands)

    lower_mine = passed_along(half(c), 1)
    energy_pair = swapped(energies)
    own, load = run(own_body, (wide(n, n), thin(n, n)), [SM, SM, VM, VM], edge[:1], at, c, ham)
    lower_theirs = swapped(lower_mine)
    one, three = row_ring(load, 1), row_ring(load, -1)
    pair, pair_half, below_c, lower_turned = run(
        pair_body, (wide(n, n), thin(n // 2, n), thin(n, n), thin(n, n)), [SM, VM, VM, VM],
        at, own, lower_mine, lower_theirs,
    )
    pair_up, pair_down = passed_along(pair_half, -1), passed_along(pair_half, 1)
    two = row_ring(one, 1)
    climb = climbed(jnp.where(x == 0, one, three))
    before, after = run(near_body, (thin(n, n),) * 2, [SM] + [VM] * 3, at, one, three, climb)
    got_before, got_after = swapped(before), swapped(after)
    got_up, got_down = swapped(pair_up), swapped(pair_down)
    chunks, first, second = run(
        second_body, (thin(parts, 2, rows, n), thin(n, n), thin(n, n)), [SM] * 4 + [VM] * 12,
        energies, inverse, edge, at, ham, pair, c, lower_turned, before, after, got_before, got_after,
        pair_up, pair_down, got_up, got_down, scratch=[pltpu.VMEM((4, n, n), jnp.bfloat16)],
    )
    first, second = flipped(first, 0), flipped(second, 1)
    received = all_to_all(chunks, ENERGY)

    got_two = swapped(two)
    extra = sent(one, [((0, 0), (1, 0))])
    near_c = sent(below_c, [((0, 0), (0, 1)), ((1, 0), (0, 3))])
    middle_c = sent(below_c, [((0, 0), (0, 2))])
    outer_ham, inner_ham, far, mid, mid_turned, near = run(
        link_body, (thin(n, n),) * 6, [SM] + [VM] * 12,
        at, c, ham, below_c, near_c, middle_c, one, two, three, got_before, got_two, got_after, extra,
    )
    outer, inner = run(role_body, (thin(n, n),) * 2, [SM, VM, VM], at, first, second)
    beyond = row_above(outer)
    beside = swapped(inner)
    open_outer, open_inner = run(
        open_body, (wide(n, n),) * 2, [SM] * 3 + [VM] * 10,
        at, energies, energy_pair, outer_ham, inner_ham, far, mid, mid_turned, near, outer, inner, beyond, beside,
    )
    result = convolved(received.reshape(count, rows, n), strength, offsets, natural, by_chip)
    self_mine = all_to_all(result, ("x", "zlo", "y")).reshape(WIDTH, pairs, rows, n)
    self_theirs = swapped(lax.dynamic_slice_in_dim(self_mine, 2 * (1 - core), 2, 0))
    mix = [pltpu.VMEM((pairs, 2, rows, n), jnp.bfloat16)]
    third = lambda role, opened, green: run(
        functools.partial(third_body, role), thin(n, n), [SM] + [VM] * 4,
        at, opened, self_mine, self_theirs, green, scratch=mix,
    )
    outer = third(False, open_outer, outer)
    beyond = row_above(outer)
    inner = third(True, open_inner, inner)
    beside = swapped(inner)
    open_outer, open_inner = run(
        part_body, (wide(n, n), wide(n, n)), [SM] * 3 + [VM] * 8, at, energies, energy_pair,
        outer_ham, inner_ham, mid, mid_turned, self_mine, self_theirs, outer, inner, scratch=mix,
    )
    whole_inner, keep_inner, give_inner = run(
        inner_body, (thin(n, n), thin(pairs, rows, n), thin(pairs, rows, n)), [SM] + [VM] * 4,
        at, near, open_inner, inner, beside, scratch=mix,
    )
    back_inner = [returned(whole_inner, True, slot) for slot in range(2)]
    got_inner = swapped(give_inner)
    whole_outer, chunks, give_outer = run(
        outer_body, (thin(n, n), thin(WIDTH, pairs, rows, n), thin(pairs, rows, n)), [SM] + [VM] * 6,
        at, far, open_outer, outer, beyond, keep_inner, got_inner, scratch=mix,
    )
    got_outer = swapped(give_outer)
    chunks = lax.dynamic_update_slice_in_dim(chunks, got_outer[None], 3 - 3 * core, 0)
    received = all_to_all(chunks.reshape(count, rows, n), ("x", "zlo", "y"))
    back_outer = [returned(whole_outer, False, slot) for slot in range(2)]
    result = convolved(received, strength, offsets, by_chip, natural)
    self_part = all_to_all(result.reshape(parts, 2, rows, n), ENERGY)
    green = run(spread_body, wide(2, n, n), [SM] + [VM] * 4, at, *back_inner, *back_outer)
    self_part = jnp.swapaxes(self_part, 0, 1).reshape(2, n, n)
    return (green[:, None], self_part[:, None])


def fine_mesh(mesh):
    energy, slab = mesh.shape["energy"], mesh.shape["slab"]
    zlo, y = (2, energy // 4) if energy > 2 else (1, 1)
    devices = mesh.devices.reshape(zlo, y, 2, slab // WIDTH, WIDTH)
    return jax.sharding.Mesh(devices, ("zlo", "y", "core", "row", "x"))


def solution(mesh):
    mesh = fine_mesh(mesh)
    return jax.shard_map(
        whole_run,
        mesh=mesh,
        in_specs=(P(ENERGY), P(SLAB), P(SLAB), P(SLAB, ENERGY), P()),
        out_specs=(P(ENERGY, SLAB), P(ENERGY, SLAB)),
        check_vma=False,
    )
```

```python
import functools

import jax
import jax.numpy as jnp
from jax import lax
from jax.experimental import pallas as pl
from jax.experimental.pallas import tpu as pltpu
from jax.sharding import PartitionSpec as P


BROAD = 0.3
REACH = 16

VM = pl.BlockSpec(memory_space=pltpu.VMEM)
SM = pl.BlockSpec(memory_space=pltpu.SMEM)


SLAB = ("row", "x")
ENERGY = ("zlo", "y", "core")
WIDTH = 4


def passed_along(value, steps):
    count = lax.axis_size(SLAB)
    leading, last = (max(0, -steps), min(count, count - steps))
    return lax.ppermute(value, SLAB, [(source, source + steps) for source in range(leading, last)])


def row_ring(value, steps):
    return lax.ppermute(value, "x", [(s, (s + steps) % WIDTH) for s in range(WIDTH)])


def swapped(value):
    return lax.ppermute(value, "core", [(0, 1), (1, 0)])


def row_above(value):
    rows = lax.axis_size("row")
    pairs = [(rows + r, r + 1) for r in range(rows - 1)] + [(r, rows + r - 1) for r in range(1, rows)]
    return lax.ppermute(value, ("core", "row"), pairs)


def crossed(value):
    rows = lax.axis_size("row")
    pairs = [(r * WIDTH - 1, r * WIDTH) for r in range(1, rows)]
    pairs += [(r * WIDTH, r * WIDTH - 1) for r in range(1, rows)]
    return lax.ppermute(value, ("core", "row", "x"), pairs)


def sent(value, pairs):
    return lax.ppermute(value, ("core", "x"), [(a * WIDTH + i, b * WIDTH + j) for (a, i), (b, j) in pairs])


def flipped(value, side):
    pairs = [(c * WIDTH + i, (i // 2) * WIDTH + 2 * c + (i % 2 + side) % 2) for c in range(2) for i in range(WIDTH)]
    return lax.ppermute(value, ("core", "x"), pairs)


def call(body, out_shape, in_specs, scratch=()):
    return pl.pallas_call(
        body,
        out_shape=out_shape,
        in_specs=in_specs,
        out_specs=jax.tree.map(lambda _: VM, out_shape),
        scratch_shapes=list(scratch),
        compiler_params=pltpu.CompilerParams(vmem_limit_bytes=16 * 1024 * 1024),
    )


def dot(a, b):
    return jnp.dot(a, b, preferred_element_type=jnp.float32)


def dot_t(a, b):
    return lax.dot_general(a, b, (((1,), (1,)), ((), ())), preferred_element_type=jnp.float32)


def tables(n):
    row = lax.broadcasted_iota(jnp.int32, (n, n), 0)
    col = lax.broadcasted_iota(jnp.int32, (n, n), 1)
    half = n // 2
    eye = jnp.where(row == col, 1.0, 0.0)
    rotate = jnp.where(col == row + half, -1.0, 0.0) + jnp.where(col == row - half, 1.0, 0.0)
    return eye, rotate


def own_body(keep_ref, at_ref, c_ref, ham_ref, own_ref, load_ref):
    own_ref[...] = dot_t(c_ref[...], c_ref[...]) * keep_ref[0]
    load_ref[...] = jnp.where(at_ref[0] == 0, ham_ref[...], c_ref[...])


def returned(value, inner, slot):
    pairs = []
    for c in range(2):
        block = (1 + c) if inner else 3 * c
        pairs += [(c * WIDTH + i, (i // 2) * WIDTH + block) for i in range(slot, WIDTH, 2)]
    return lax.ppermute(value, ("core", "x"), pairs)


def place_halves(core, whole, mine, theirs):
    half = mine.shape[0]
    whole[pl.ds(pl.multiple_of(core * half, half), half)] = mine
    whole[pl.ds(pl.multiple_of((1 - core) * half, half), half)] = theirs


def pair_body(at_ref, own_ref, mine_ref, theirs_ref, pair_ref, half_ref, below_ref, turned_ref):
    core = at_ref[0]
    half = half_ref.shape[0]
    place_halves(core, below_ref, mine_ref[...], theirs_ref[...])
    below = below_ref[...]
    turned = below.T
    turned_ref[...] = turned
    pair_ref[...] = own_ref[...] + dot(turned, below)
    half_ref[...] = pair_ref[pl.ds(pl.multiple_of(core * half, half), half)].astype(jnp.bfloat16)


def first_step(energy, inverse, ham, pair, eye):
    square = inverse * inverse
    return (
        (square * inverse) * pair.astype(jnp.float32) + square * ham + (2.0 * inverse - square * energy) * eye
    ).astype(jnp.bfloat16)


def linked(green, link):
    return dot(link, dot_t(green, link).astype(jnp.bfloat16))


def finish(matrix, green, eye):
    product = dot(matrix, green)
    residue = (2.0 * eye - product).astype(jnp.bfloat16)
    return dot(green, residue)


def near_body(at_ref, one_ref, three_ref, crossed_ref, previous_ref, next_ref):
    first = at_ref[0] == 0
    previous_ref[...] = jnp.where(jnp.logical_and(first, at_ref[1] == 0), crossed_ref[...], one_ref[...])
    next_ref[...] = jnp.where(jnp.logical_and(first, at_ref[1] == WIDTH - 1), crossed_ref[...], three_ref[...])


def second_body(
    energy_ref, inverse_ref, edge_ref, at_ref, ham_ref, pair_ref, c_ref, lower_turned_ref, previous_ref, next_ref,
    got_previous_ref, got_next_ref, up_ref, down_ref, got_up_ref, got_down_ref, out_ref, first_ref, second_ref, whole,
):
    n = c_ref.shape[0]
    eye, rotate = tables(n)
    chunks = out_ref.shape[0]
    first = at_ref[0] == 0
    whole[0] = jnp.where(first, next_ref[...], got_next_ref[...])
    whole[1] = jnp.where(first, previous_ref[...], got_previous_ref[...])
    place_halves(at_ref[0], whole.at[2], up_ref[...], got_up_ref[...])
    place_halves(at_ref[0], whole.at[3], down_ref[...], got_down_ref[...])
    odd = lax.rem(at_ref[1], 2)
    turn = BROAD * rotate
    ham = ham_ref[...].astype(jnp.float32) - turn
    ham_above = whole[0].astype(jnp.float32) - turn
    ham_below = whole[1].astype(jnp.float32) - turn
    for e, same_ref in ((odd, first_ref), (1 - odd, second_ref)):
        energy, inverse = energy_ref[e], inverse_ref[e]
        above = first_step(energy, inverse * edge_ref[0], ham_above, whole[2], eye)
        below = first_step(energy, inverse * edge_ref[1], ham_below, whole[3], eye)
        green = first_step(energy, inverse, ham, pair_ref[...], eye)
        terms = linked(above, c_ref[...]) + linked(below, lower_turned_ref[...])
        matrix = (energy * eye - ham - terms).astype(jnp.bfloat16)
        result = finish(matrix, green, eye).astype(jnp.bfloat16)
        out_ref[:, e] = result.reshape(chunks, n // chunks, n)
        same_ref[...] = result


def link_body(
    at_ref, c_ref, ham_ref, below_ref, near_ref, middle_ref, mine_1, mine_2, mine_3, other_1, other_2, other_3, extra,
    outer_ham, inner_ham, far, mid, mid_turned, near,
):
    x = at_ref[1]

    def block(b, here, one, two, three):
        k = lax.rem(x + WIDTH - b, WIDTH)
        return jnp.where(k == 0, here, jnp.where(k == 1, one, jnp.where(k == 2, two, three)))

    @pl.when(at_ref[0] == 0)
    def _():
        hams = (ham_ref[...], mine_1[...], mine_2[...], mine_3[...])
        links = (c_ref[...], other_1[...], other_2[...], other_3[...])
        outer_ham[...] = block(0, *hams)
        inner_ham[...] = block(1, *hams)
        far[...] = jnp.where(x == 0, below_ref[...], jnp.where(x == 2, middle_ref[...], near_ref[...])).T
        middle = block(0, *links)
        mid[...] = middle
        mid_turned[...] = middle.T
        near[...] = block(1, *links)

    @pl.when(at_ref[0] == 1)
    def _():
        hams = (ham_ref[...], jnp.where(x == 0, extra[...], other_1[...]), other_2[...], other_3[...])
        links = (c_ref[...], mine_1[...], mine_2[...], mine_3[...])
        outer_ham[...] = block(3, *hams)
        inner_ham[...] = block(2, *hams)
        far[...] = block(3, *links)
        middle = block(2, *links)
        mid[...] = middle.T
        mid_turned[...] = middle
        near[...] = block(1, *links).T


def row_energy(at_ref, energy_ref, pair_ref):
    core, x = at_ref[0], at_ref[1]
    return jnp.where(x // 2 == core, energy_ref[lax.rem(x, 2)], pair_ref[lax.rem(x, 2)])


def role_body(at_ref, first_ref, second_ref, outer_ref, inner_ref):
    match = lax.rem(at_ref[1], 2) == at_ref[0]
    outer_ref[...] = jnp.where(match, first_ref[...], second_ref[...])
    inner_ref[...] = jnp.where(match, second_ref[...], first_ref[...])


def open_body(
    at_ref, energy_ref, energy_pair_ref, outer_ham, inner_ham, far, mid, mid_turned, near, outer, inner, beyond, beside, open_outer, open_inner,
):
    eye, rotate = tables(outer.shape[0])
    base = row_energy(at_ref, energy_ref, energy_pair_ref) * eye + BROAD * rotate
    open_outer[...] = (
        base - outer_ham[...].astype(jnp.float32) - linked(inner[...], mid[...]) - linked(beyond[...], far[...])
    )
    open_inner[...] = (
        base - inner_ham[...].astype(jnp.float32) - linked(outer[...], mid_turned[...]) - linked(beside[...], near[...])
    )


def joined_rows(core, slot, mine_ref, theirs_ref, scratch):
    scratch[:, core] = mine_ref[2 * core + slot]
    scratch[:, 1 - core] = theirs_ref[slot]
    n = scratch.shape[-1]
    return scratch[...].reshape(n, n).astype(jnp.float32)


def third_body(inner, at_ref, open_ref, mine_ref, theirs_ref, green_ref, out_ref, scratch):
    core = at_ref[0]
    eye, _ = tables(open_ref.shape[0])
    self_part = joined_rows(core, 1 - core if inner else core, mine_ref, theirs_ref, scratch)
    matrix = (open_ref[...] - self_part).astype(jnp.bfloat16)
    out_ref[...] = finish(matrix, green_ref[...], eye).astype(jnp.bfloat16)


def split_rows(core, result, keep_ref, give_ref, scratch):
    scratch[...] = result.reshape(scratch.shape)
    keep_ref[...] = scratch[:, core]
    give_ref[...] = scratch[:, 1 - core]


def part_body(
    at_ref, energy_ref, energy_pair_ref, outer_ham, inner_ham, mid, mid_turned, mine_ref, theirs_ref, outer, inner,
    open_outer, open_inner, scratch,
):
    core = at_ref[0]
    eye, rotate = tables(outer.shape[0])
    base = row_energy(at_ref, energy_ref, energy_pair_ref) * eye + BROAD * rotate
    self_part = joined_rows(core, 1 - core, mine_ref, theirs_ref, scratch)
    open_inner[...] = base - inner_ham[...].astype(jnp.float32) - self_part - linked(outer[...], mid_turned[...])
    self_part = joined_rows(core, core, mine_ref, theirs_ref, scratch)
    open_outer[...] = base - outer_ham[...].astype(jnp.float32) - self_part - linked(inner[...], mid[...])


def inner_body(at_ref, near, open_ref, inner, beside, whole_ref, keep_ref, give_ref, scratch):
    eye, _ = tables(inner.shape[0])
    matrix = (open_ref[...] - linked(beside[...], near[...])).astype(jnp.bfloat16)
    result = finish(matrix, inner[...], eye).astype(jnp.bfloat16)
    whole_ref[...] = result
    split_rows(at_ref[0], result, keep_ref, give_ref, scratch)


def outer_body(
    at_ref, far, open_ref, outer, beyond, keep_inner, got_inner, whole_ref, out_ref, give_ref, scratch
):
    core = at_ref[0]
    eye, _ = tables(outer.shape[0])
    matrix = (open_ref[...] - linked(beyond[...], far[...])).astype(jnp.bfloat16)
    result = finish(matrix, outer[...], eye).astype(jnp.bfloat16)
    whole_ref[...] = result
    scratch[...] = result.reshape(scratch.shape)
    give_ref[...] = scratch[:, 1 - core]
    out_ref[3 * core] = scratch[:, core]
    out_ref[1 + core] = keep_inner[...]
    out_ref[2 - core] = got_inner[...]
    out_ref[3 - 3 * core] = got_inner[...]


def spread_body(at_ref, inner_0, inner_1, outer_0, outer_1, out_ref):
    within = jnp.logical_and(at_ref[1] > 0, at_ref[1] < WIDTH - 1)
    out_ref[0] = jnp.where(within, inner_0[...], outer_0[...]).astype(jnp.float32)
    out_ref[1] = jnp.where(within, inner_1[...], outer_1[...]).astype(jnp.float32)


def energy_body(place_in, place_out, offset_ref, green_ref, coulomb_ref, out_ref, padded):
    count, rows, columns = green_ref.shape
    offset_count = offset_ref.shape[0]
    none = jnp.zeros((REACH, 8, 128), jnp.float32)
    padded[:REACH] = none
    padded[REACH + count :] = none
    column_tiles = columns // 128

    def tile(t, carry):
        row = pl.ds(pl.multiple_of(8 * (t // column_tiles), 8), 8)
        column = pl.ds(pl.multiple_of(128 * (t % column_tiles), 128), 128)
        strength = coulomb_ref[row, column].astype(jnp.float32)
        own = [green_ref[place_in[e], row, column].astype(jnp.float32) for e in range(count)]
        for e in range(count):
            padded[REACH + e] = own[e]
        screened = []
        for k in range(offset_count):
            later = padded.at[pl.ds(REACH + offset_ref[k], count)]
            sums = [own[e] * later[e] for e in range(4)]
            for e in range(4, count):
                sums[e % 4] = sums[e % 4] + own[e] * later[e]
            polarization = (4.0 / count) * ((sums[0] + sums[1]) + (sums[2] + sums[3]))
            screened.append(strength * (1.0 + polarization * strength) * (1.0 / offset_count))
        earlier = [padded.at[pl.ds(REACH - offset_ref[k], count)] for k in range(offset_count)]
        for e in range(count):
            terms = [screened[k] * earlier[k][e] for k in range(offset_count)]
            while len(terms) > 1:
                terms = [a + b for a, b in zip(terms[::2], terms[1::2])] + terms[len(terms) // 2 * 2 :]
            out_ref[place_out[e], row, column] = terms[0].astype(jnp.bfloat16)
        return carry

    lax.fori_loop(0, (rows // 8) * column_tiles, tile, 0)


def convolved(received, coulomb, offsets, place_in, place_out):
    count, rows, columns = received.shape
    return call(
        functools.partial(energy_body, place_in, place_out),
        jax.ShapeDtypeStruct((count, rows, columns), jnp.bfloat16),
        [SM, VM, VM],
        [pltpu.VMEM((count + 2 * REACH, 8, 128), jnp.float32)],
    )(offsets, received, coulomb)


def all_to_all(value, axes):
    return lax.all_to_all(value, axes, split_axis=0, concat_axis=0, tiled=True)


def whole_run(energies, hamiltonian, coupling, coulomb, offsets):
    c, ham, strength = coupling[0], hamiltonian[0], coulomb[0]
    n = c.shape[0]
    parts = lax.axis_size(ENERGY)
    rows, pairs = n // parts, parts // 2
    count = 2 * parts
    place, x, core = lax.axis_index(SLAB), lax.axis_index("x"), lax.axis_index("core")
    edge = jnp.stack([place < lax.axis_size(SLAB) - 1, place > 0]).astype(jnp.float32)
    at = jnp.stack([core, x]).astype(jnp.int32)
    inverse = (1.0 / energies).astype(jnp.bfloat16).astype(jnp.float32)
    half = lambda value: lax.dynamic_slice_in_dim(value, core * (n // 2), n // 2, 0)
    wide = lambda *dims: jax.ShapeDtypeStruct(dims, jnp.float32)
    thin = lambda *dims: jax.ShapeDtypeStruct(dims, jnp.bfloat16)
    natural = list(range(count))
    by_chip = [(e % WIDTH) * (count // WIDTH) + e // WIDTH for e in range(count)]

    def run(body, out_shape, in_specs, *operands, scratch=()):
        return call(body, out_shape, in_specs, scratch)(*operands)

    lower_mine = passed_along(half(c), 1)
    energy_pair = swapped(energies)
    own, load = run(own_body, (wide(n, n), thin(n, n)), [SM, SM, VM, VM], edge[:1], at, c, ham)
    lower_theirs = swapped(lower_mine)
    one, three = row_ring(load, 1), row_ring(load, -1)
    crossing = crossed(ham)
    pair, pair_half, below_c, lower_turned = run(
        pair_body, (wide(n, n), thin(n // 2, n), thin(n, n), thin(n, n)), [SM, VM, VM, VM],
        at, own, lower_mine, lower_theirs,
    )
    pair_up, pair_down = passed_along(pair_half, -1), passed_along(pair_half, 1)
    two = row_ring(one, 1)
    before, after = run(near_body, (thin(n, n),) * 2, [SM] + [VM] * 3, at, one, three, crossing)
    got_before, got_after = swapped(before), swapped(after)
    got_up, got_down = swapped(pair_up), swapped(pair_down)
    chunks, first, second = run(
        second_body, (thin(parts, 2, rows, n), thin(n, n), thin(n, n)), [SM] * 4 + [VM] * 12,
        energies, inverse, edge, at, ham, pair, c, lower_turned, before, after, got_before, got_after,
        pair_up, pair_down, got_up, got_down, scratch=[pltpu.VMEM((4, n, n), jnp.bfloat16)],
    )
    first, second = flipped(first, 0), flipped(second, 1)
    received = all_to_all(chunks, ENERGY)

    got_two = swapped(two)
    extra = sent(one, [((0, 0), (1, 0))])
    near_c = sent(below_c, [((0, 0), (0, 1)), ((1, 0), (0, 3))])
    middle_c = sent(below_c, [((0, 0), (0, 2))])
    outer_ham, inner_ham, far, mid, mid_turned, near = run(
        link_body, (thin(n, n),) * 6, [SM] + [VM] * 12,
        at, c, ham, below_c, near_c, middle_c, one, two, three, got_before, got_two, got_after, extra,
    )
    outer, inner = run(role_body, (thin(n, n),) * 2, [SM, VM, VM], at, first, second)
    beyond = row_above(outer)
    beside = swapped(inner)
    open_outer, open_inner = run(
        open_body, (wide(n, n),) * 2, [SM] * 3 + [VM] * 10,
        at, energies, energy_pair, outer_ham, inner_ham, far, mid, mid_turned, near, outer, inner, beyond, beside,
    )
    result = convolved(received.reshape(count, rows, n), strength, offsets, natural, by_chip)
    self_mine = all_to_all(result, ("x", "zlo", "y")).reshape(WIDTH, pairs, rows, n)
    self_theirs = swapped(lax.dynamic_slice_in_dim(self_mine, 2 * (1 - core), 2, 0))
    mix = [pltpu.VMEM((pairs, 2, rows, n), jnp.bfloat16)]
    third = lambda role, opened, green: run(
        functools.partial(third_body, role), thin(n, n), [SM] + [VM] * 4,
        at, opened, self_mine, self_theirs, green, scratch=mix,
    )
    outer = third(False, open_outer, outer)
    beyond = row_above(outer)
    inner = third(True, open_inner, inner)
    beside = swapped(inner)
    open_outer, open_inner = run(
        part_body, (wide(n, n), wide(n, n)), [SM] * 3 + [VM] * 8, at, energies, energy_pair,
        outer_ham, inner_ham, mid, mid_turned, self_mine, self_theirs, outer, inner, scratch=mix,
    )
    whole_inner, keep_inner, give_inner = run(
        inner_body, (thin(n, n), thin(pairs, rows, n), thin(pairs, rows, n)), [SM] + [VM] * 4,
        at, near, open_inner, inner, beside, scratch=mix,
    )
    back_inner = [returned(whole_inner, True, slot) for slot in range(2)]
    got_inner = swapped(give_inner)
    whole_outer, chunks, give_outer = run(
        outer_body, (thin(n, n), thin(WIDTH, pairs, rows, n), thin(pairs, rows, n)), [SM] + [VM] * 6,
        at, far, open_outer, outer, beyond, keep_inner, got_inner, scratch=mix,
    )
    got_outer = swapped(give_outer)
    chunks = lax.dynamic_update_slice_in_dim(chunks, got_outer[None], 3 - 3 * core, 0)
    received = all_to_all(chunks.reshape(count, rows, n), ("x", "zlo", "y"))
    back_outer = [returned(whole_outer, False, slot) for slot in range(2)]
    result = convolved(received, strength, offsets, by_chip, natural)
    self_part = all_to_all(result.reshape(parts, 2, rows, n), ENERGY)
    green = run(spread_body, wide(2, n, n), [SM] + [VM] * 4, at, *back_inner, *back_outer)
    self_part = jnp.swapaxes(self_part, 0, 1).reshape(2, n, n)
    return (green[:, None], self_part[:, None])


def fine_mesh(mesh):
    energy, slab = mesh.shape["energy"], mesh.shape["slab"]
    zlo, y = (2, energy // 4) if energy > 2 else (1, 1)
    devices = mesh.devices.reshape(zlo, y, 2, slab // WIDTH, WIDTH)
    return jax.sharding.Mesh(devices, ("zlo", "y", "core", "row", "x"))


def solution(mesh):
    mesh = fine_mesh(mesh)
    return jax.shard_map(
        whole_run,
        mesh=mesh,
        in_specs=(P(ENERGY), P(SLAB), P(SLAB), P(SLAB, ENERGY), P()),
        out_specs=(P(ENERGY, SLAB), P(ENERGY, SLAB)),
        check_vma=False,
    )
```

```python
import functools

import jax
import jax.numpy as jnp
from jax import lax
from jax.experimental import pallas as pl
from jax.experimental.pallas import tpu as pltpu
from jax.sharding import PartitionSpec as P


BROAD = 0.3
REACH = 16

VM = pl.BlockSpec(memory_space=pltpu.VMEM)
SM = pl.BlockSpec(memory_space=pltpu.SMEM)


SLAB = ("row", "x")
ENERGY = ("zlo", "y", "core")
WIDTH = 4


def passed_along(value, steps):
    count = lax.axis_size(SLAB)
    leading, last = (max(0, -steps), min(count, count - steps))
    return lax.ppermute(value, SLAB, [(source, source + steps) for source in range(leading, last)])


def row_ring(value, steps):
    return lax.ppermute(value, "x", [(s, (s + steps) % WIDTH) for s in range(WIDTH)])


def swapped(value):
    return lax.ppermute(value, "core", [(0, 1), (1, 0)])


def row_above(value):
    rows = lax.axis_size("row")
    pairs = [(rows + r, r + 1) for r in range(rows - 1)] + [(r, rows + r - 1) for r in range(1, rows)]
    return lax.ppermute(value, ("core", "row"), pairs)


def crossed(value):
    rows = lax.axis_size("row")
    pairs = [(r * WIDTH - 1, r * WIDTH) for r in range(1, rows)]
    pairs += [(r * WIDTH, r * WIDTH - 1) for r in range(1, rows)]
    return lax.ppermute(value, ("core", "row", "x"), pairs)


def sent(value, pairs):
    return lax.ppermute(value, ("core", "x"), [(a * WIDTH + i, b * WIDTH + j) for (a, i), (b, j) in pairs])


def flipped(value, side):
    pairs = [(c * WIDTH + i, (i // 2) * WIDTH + 2 * c + (i % 2 + side) % 2) for c in range(2) for i in range(WIDTH)]
    return lax.ppermute(value, ("core", "x"), pairs)


def call(body, out_shape, in_specs, scratch=()):
    return pl.pallas_call(
        body,
        out_shape=out_shape,
        in_specs=in_specs,
        out_specs=jax.tree.map(lambda _: VM, out_shape),
        scratch_shapes=list(scratch),
        compiler_params=pltpu.CompilerParams(vmem_limit_bytes=16 * 1024 * 1024),
    )


def dot(a, b):
    return jnp.dot(a, b, preferred_element_type=jnp.float32)


def dot_t(a, b):
    return lax.dot_general(a, b, (((1,), (1,)), ((), ())), preferred_element_type=jnp.float32)


def tables(n):
    row = lax.broadcasted_iota(jnp.int32, (n, n), 0)
    col = lax.broadcasted_iota(jnp.int32, (n, n), 1)
    half = n // 2
    eye = jnp.where(row == col, 1.0, 0.0)
    rotate = jnp.where(col == row + half, -1.0, 0.0) + jnp.where(col == row - half, 1.0, 0.0)
    return eye, rotate


def own_body(keep_ref, at_ref, c_ref, ham_ref, own_ref, load_ref):
    own_ref[...] = dot_t(c_ref[...], c_ref[...]) * keep_ref[0]
    load_ref[...] = jnp.where(at_ref[0] == 0, ham_ref[...], c_ref[...])


def returned(value, inner, slot):
    pairs = []
    for c in range(2):
        block = (1 + c) if inner else 3 * c
        pairs += [(c * WIDTH + i, (i // 2) * WIDTH + block) for i in range(slot, WIDTH, 2)]
    return lax.ppermute(value, ("core", "x"), pairs)


def place_halves(core, whole, mine, theirs):
    half = mine.shape[0]
    whole[pl.ds(pl.multiple_of(core * half, half), half)] = mine
    whole[pl.ds(pl.multiple_of((1 - core) * half, half), half)] = theirs


def pair_body(at_ref, own_ref, mine_ref, theirs_ref, pair_ref, half_ref, below_ref, turned_ref):
    core = at_ref[0]
    half = half_ref.shape[0]
    place_halves(core, below_ref, mine_ref[...], theirs_ref[...])
    below = below_ref[...]
    turned = below.T
    turned_ref[...] = turned
    pair_ref[...] = own_ref[...] + dot(turned, below)
    half_ref[...] = pair_ref[pl.ds(pl.multiple_of(core * half, half), half)].astype(jnp.bfloat16)


def above_body(keep_ref, at_ref, c_ref, mine_ref, theirs_ref, out_ref, whole):
    place_halves(at_ref[0], whole, mine_ref[...], theirs_ref[...])
    out_ref[...] = dot_t(whole[...], whole[...]) * keep_ref[0] + dot(c_ref[...].T, c_ref[...])


def first_step(energy, inverse, ham, pair, eye):
    square = inverse * inverse
    return (
        (square * inverse) * pair.astype(jnp.float32) + square * ham + (2.0 * inverse - square * energy) * eye
    ).astype(jnp.bfloat16)


def linked(green, link):
    return dot(link, dot_t(green, link).astype(jnp.bfloat16))


def finish(matrix, green, eye):
    product = dot(matrix, green)
    residue = (2.0 * eye - product).astype(jnp.bfloat16)
    return dot(green, residue)


def near_body(at_ref, one_ref, three_ref, crossed_ref, previous_ref, next_ref):
    first = at_ref[0] == 0
    previous_ref[...] = jnp.where(jnp.logical_and(first, at_ref[1] == 0), crossed_ref[...], one_ref[...])
    next_ref[...] = jnp.where(jnp.logical_and(first, at_ref[1] == WIDTH - 1), crossed_ref[...], three_ref[...])


def second_body(
    energy_ref, inverse_ref, edge_ref, at_ref, ham_ref, pair_ref, c_ref, lower_turned_ref, previous_ref, next_ref,
    got_previous_ref, got_next_ref, above_ref, down_ref, got_down_ref, out_ref, first_ref, second_ref, whole,
):
    n = c_ref.shape[0]
    eye, rotate = tables(n)
    chunks = out_ref.shape[0]
    first = at_ref[0] == 0
    whole[0] = jnp.where(first, next_ref[...], got_next_ref[...])
    whole[1] = jnp.where(first, previous_ref[...], got_previous_ref[...])
    place_halves(at_ref[0], whole.at[2], down_ref[...], got_down_ref[...])
    odd = lax.rem(at_ref[1], 2)
    turn = BROAD * rotate
    ham = ham_ref[...].astype(jnp.float32) - turn
    ham_above = whole[0].astype(jnp.float32) - turn
    ham_below = whole[1].astype(jnp.float32) - turn
    for e, same_ref in ((odd, first_ref), (1 - odd, second_ref)):
        energy, inverse = energy_ref[e], inverse_ref[e]
        above = first_step(energy, inverse * edge_ref[0], ham_above, above_ref[...], eye)
        below = first_step(energy, inverse * edge_ref[1], ham_below, whole[2], eye)
        green = first_step(energy, inverse, ham, pair_ref[...], eye)
        terms = linked(above, c_ref[...]) + linked(below, lower_turned_ref[...])
        matrix = (energy * eye - ham - terms).astype(jnp.bfloat16)
        result = finish(matrix, green, eye).astype(jnp.bfloat16)
        out_ref[:, e] = result.reshape(chunks, n // chunks, n)
        same_ref[...] = result


def link_body(
    at_ref, c_ref, ham_ref, below_ref, near_ref, middle_ref, mine_1, mine_2, mine_3, other_1, other_2, other_3, extra,
    outer_ham, inner_ham, far, mid, mid_turned, near,
):
    x = at_ref[1]

    def block(b, here, one, two, three):
        k = lax.rem(x + WIDTH - b, WIDTH)
        return jnp.where(k == 0, here, jnp.where(k == 1, one, jnp.where(k == 2, two, three)))

    @pl.when(at_ref[0] == 0)
    def _():
        hams = (ham_ref[...], mine_1[...], mine_2[...], mine_3[...])
        links = (c_ref[...], other_1[...], other_2[...], other_3[...])
        outer_ham[...] = block(0, *hams)
        inner_ham[...] = block(1, *hams)
        far[...] = jnp.where(x == 0, below_ref[...], jnp.where(x == 2, middle_ref[...], near_ref[...])).T
        middle = block(0, *links)
        mid[...] = middle
        mid_turned[...] = middle.T
        near[...] = block(1, *links)

    @pl.when(at_ref[0] == 1)
    def _():
        hams = (ham_ref[...], jnp.where(x == 0, extra[...], other_1[...]), other_2[...], other_3[...])
        links = (c_ref[...], mine_1[...], mine_2[...], mine_3[...])
        outer_ham[...] = block(3, *hams)
        inner_ham[...] = block(2, *hams)
        far[...] = block(3, *links)
        middle = block(2, *links)
        mid[...] = middle.T
        mid_turned[...] = middle
        near[...] = block(1, *links).T


def row_energy(at_ref, energy_ref, pair_ref):
    core, x = at_ref[0], at_ref[1]
    return jnp.where(x // 2 == core, energy_ref[lax.rem(x, 2)], pair_ref[lax.rem(x, 2)])


def role_body(at_ref, first_ref, second_ref, outer_ref, inner_ref):
    match = lax.rem(at_ref[1], 2) == at_ref[0]
    outer_ref[...] = jnp.where(match, first_ref[...], second_ref[...])
    inner_ref[...] = jnp.where(match, second_ref[...], first_ref[...])


def open_body(
    at_ref, energy_ref, energy_pair_ref, outer_ham, inner_ham, far, mid, mid_turned, near, outer, inner, beyond, beside, open_outer, open_inner,
):
    eye, rotate = tables(outer.shape[0])
    base = row_energy(at_ref, energy_ref, energy_pair_ref) * eye + BROAD * rotate
    open_outer[...] = (
        base - outer_ham[...].astype(jnp.float32) - linked(inner[...], mid[...]) - linked(beyond[...], far[...])
    )
    open_inner[...] = (
        base - inner_ham[...].astype(jnp.float32) - linked(outer[...], mid_turned[...]) - linked(beside[...], near[...])
    )


def joined_rows(core, slot, mine_ref, theirs_ref, scratch):
    scratch[:, core] = mine_ref[2 * core + slot]
    scratch[:, 1 - core] = theirs_ref[slot]
    n = scratch.shape[-1]
    return scratch[...].reshape(n, n).astype(jnp.float32)


def third_body(inner, at_ref, open_ref, mine_ref, theirs_ref, green_ref, out_ref, scratch):
    core = at_ref[0]
    eye, _ = tables(open_ref.shape[0])
    self_part = joined_rows(core, 1 - core if inner else core, mine_ref, theirs_ref, scratch)
    matrix = (open_ref[...] - self_part).astype(jnp.bfloat16)
    out_ref[...] = finish(matrix, green_ref[...], eye).astype(jnp.bfloat16)


def split_rows(core, result, keep_ref, give_ref, scratch):
    scratch[...] = result.reshape(scratch.shape)
    keep_ref[...] = scratch[:, core]
    give_ref[...] = scratch[:, 1 - core]


def part_body(
    at_ref, energy_ref, energy_pair_ref, outer_ham, inner_ham, mid, mid_turned, mine_ref, theirs_ref, outer, inner,
    open_outer, open_inner, scratch,
):
    core = at_ref[0]
    eye, rotate = tables(outer.shape[0])
    base = row_energy(at_ref, energy_ref, energy_pair_ref) * eye + BROAD * rotate
    self_part = joined_rows(core, 1 - core, mine_ref, theirs_ref, scratch)
    open_inner[...] = base - inner_ham[...].astype(jnp.float32) - self_part - linked(outer[...], mid_turned[...])
    self_part = joined_rows(core, core, mine_ref, theirs_ref, scratch)
    open_outer[...] = base - outer_ham[...].astype(jnp.float32) - self_part - linked(inner[...], mid[...])


def inner_body(at_ref, near, open_ref, inner, beside, whole_ref, keep_ref, give_ref, scratch):
    eye, _ = tables(inner.shape[0])
    matrix = (open_ref[...] - linked(beside[...], near[...])).astype(jnp.bfloat16)
    result = finish(matrix, inner[...], eye).astype(jnp.bfloat16)
    whole_ref[...] = result
    split_rows(at_ref[0], result, keep_ref, give_ref, scratch)


def outer_body(
    at_ref, far, open_ref, outer, beyond, keep_inner, got_inner, whole_ref, out_ref, give_ref, scratch
):
    core = at_ref[0]
    eye, _ = tables(outer.shape[0])
    matrix = (open_ref[...] - linked(beyond[...], far[...])).astype(jnp.bfloat16)
    result = finish(matrix, outer[...], eye).astype(jnp.bfloat16)
    whole_ref[...] = result
    scratch[...] = result.reshape(scratch.shape)
    give_ref[...] = scratch[:, 1 - core]
    out_ref[3 * core] = scratch[:, core]
    out_ref[1 + core] = keep_inner[...]
    out_ref[2 - core] = got_inner[...]
    out_ref[3 - 3 * core] = got_inner[...]


def spread_body(at_ref, inner_0, inner_1, outer_0, outer_1, out_ref):
    within = jnp.logical_and(at_ref[1] > 0, at_ref[1] < WIDTH - 1)
    out_ref[0] = jnp.where(within, inner_0[...], outer_0[...]).astype(jnp.float32)
    out_ref[1] = jnp.where(within, inner_1[...], outer_1[...]).astype(jnp.float32)


def energy_body(place_in, place_out, offset_ref, green_ref, coulomb_ref, out_ref, padded):
    count, rows, columns = green_ref.shape
    offset_count = offset_ref.shape[0]
    none = jnp.zeros((REACH, 8, 128), jnp.float32)
    padded[:REACH] = none
    padded[REACH + count :] = none
    column_tiles = columns // 128

    def tile(t, carry):
        row = pl.ds(pl.multiple_of(8 * (t // column_tiles), 8), 8)
        column = pl.ds(pl.multiple_of(128 * (t % column_tiles), 128), 128)
        strength = coulomb_ref[row, column].astype(jnp.float32)
        own = [green_ref[place_in[e], row, column].astype(jnp.float32) for e in range(count)]
        for e in range(count):
            padded[REACH + e] = own[e]
        screened = []
        for k in range(offset_count):
            later = padded.at[pl.ds(REACH + offset_ref[k], count)]
            sums = [own[e] * later[e] for e in range(4)]
            for e in range(4, count):
                sums[e % 4] = sums[e % 4] + own[e] * later[e]
            polarization = (4.0 / count) * ((sums[0] + sums[1]) + (sums[2] + sums[3]))
            screened.append(strength * (1.0 + polarization * strength) * (1.0 / offset_count))
        earlier = [padded.at[pl.ds(REACH - offset_ref[k], count)] for k in range(offset_count)]
        for e in range(count):
            terms = [screened[k] * earlier[k][e] for k in range(offset_count)]
            while len(terms) > 1:
                terms = [a + b for a, b in zip(terms[::2], terms[1::2])] + terms[len(terms) // 2 * 2 :]
            out_ref[place_out[e], row, column] = terms[0].astype(jnp.bfloat16)
        return carry

    lax.fori_loop(0, (rows // 8) * column_tiles, tile, 0)


def convolved(received, coulomb, offsets, place_in, place_out):
    count, rows, columns = received.shape
    return call(
        functools.partial(energy_body, place_in, place_out),
        jax.ShapeDtypeStruct((count, rows, columns), jnp.bfloat16),
        [SM, VM, VM],
        [pltpu.VMEM((count + 2 * REACH, 8, 128), jnp.float32)],
    )(offsets, received, coulomb)


def all_to_all(value, axes):
    return lax.all_to_all(value, axes, split_axis=0, concat_axis=0, tiled=True)


def whole_run(energies, hamiltonian, coupling, coulomb, offsets):
    c, ham, strength = coupling[0], hamiltonian[0], coulomb[0]
    n = c.shape[0]
    parts = lax.axis_size(ENERGY)
    rows, pairs = n // parts, parts // 2
    count = 2 * parts
    place, x, core = lax.axis_index(SLAB), lax.axis_index("x"), lax.axis_index("core")
    edge = jnp.stack([place < lax.axis_size(SLAB) - 1, place > 0, place < lax.axis_size(SLAB) - 2]).astype(jnp.float32)
    at = jnp.stack([core, x]).astype(jnp.int32)
    inverse = (1.0 / energies).astype(jnp.bfloat16).astype(jnp.float32)
    half = lambda value: lax.dynamic_slice_in_dim(value, core * (n // 2), n // 2, 0)
    wide = lambda *dims: jax.ShapeDtypeStruct(dims, jnp.float32)
    thin = lambda *dims: jax.ShapeDtypeStruct(dims, jnp.bfloat16)
    natural = list(range(count))
    by_chip = [(e % WIDTH) * (count // WIDTH) + e // WIDTH for e in range(count)]

    def run(body, out_shape, in_specs, *operands, scratch=()):
        return call(body, out_shape, in_specs, scratch)(*operands)

    c_half = half(c)
    lower_mine = passed_along(c_half, 1)
    upper_mine = passed_along(c_half, -1)
    energy_pair = swapped(energies)
    own, load = run(own_body, (wide(n, n), thin(n, n)), [SM, SM, VM, VM], edge[:1], at, c, ham)
    lower_theirs = swapped(lower_mine)
    one, three = row_ring(load, 1), row_ring(load, -1)
    crossing = crossed(ham)
    pair, pair_half, below_c, lower_turned = run(
        pair_body, (wide(n, n), thin(n // 2, n), thin(n, n), thin(n, n)), [SM, VM, VM, VM],
        at, own, lower_mine, lower_theirs,
    )
    pair_down = passed_along(pair_half, 1)
    upper_theirs = swapped(upper_mine)
    above = run(
        above_body, wide(n, n), [SM, SM, VM, VM, VM], edge[2:], at, c, upper_mine, upper_theirs,
        scratch=[pltpu.VMEM((n, n), jnp.bfloat16)],
    )
    two = row_ring(one, 1)
    before, after = run(near_body, (thin(n, n),) * 2, [SM] + [VM] * 3, at, one, three, crossing)
    got_before, got_after = swapped(before), swapped(after)
    got_down = swapped(pair_down)
    chunks, first, second = run(
        second_body, (thin(parts, 2, rows, n), thin(n, n), thin(n, n)), [SM] * 4 + [VM] * 11,
        energies, inverse, edge, at, ham, pair, c, lower_turned, before, after, got_before, got_after,
        above, pair_down, got_down, scratch=[pltpu.VMEM((3, n, n), jnp.bfloat16)],
    )
    first, second = flipped(first, 0), flipped(second, 1)
    received = all_to_all(chunks, ENERGY)

    got_two = swapped(two)
    extra = sent(one, [((0, 0), (1, 0))])
    near_c = sent(below_c, [((0, 0), (0, 1)), ((1, 0), (0, 3))])
    middle_c = sent(below_c, [((0, 0), (0, 2))])
    outer_ham, inner_ham, far, mid, mid_turned, near = run(
        link_body, (thin(n, n),) * 6, [SM] + [VM] * 12,
        at, c, ham, below_c, near_c, middle_c, one, two, three, got_before, got_two, got_after, extra,
    )
    outer, inner = run(role_body, (thin(n, n),) * 2, [SM, VM, VM], at, first, second)
    beyond = row_above(outer)
    beside = swapped(inner)
    open_outer, open_inner = run(
        open_body, (wide(n, n),) * 2, [SM] * 3 + [VM] * 10,
        at, energies, energy_pair, outer_ham, inner_ham, far, mid, mid_turned, near, outer, inner, beyond, beside,
    )
    result = convolved(received.reshape(count, rows, n), strength, offsets, natural, by_chip)
    self_mine = all_to_all(result, ("x", "zlo", "y")).reshape(WIDTH, pairs, rows, n)
    self_theirs = swapped(lax.dynamic_slice_in_dim(self_mine, 2 * (1 - core), 2, 0))
    mix = [pltpu.VMEM((pairs, 2, rows, n), jnp.bfloat16)]
    third = lambda role, opened, green: run(
        functools.partial(third_body, role), thin(n, n), [SM] + [VM] * 4,
        at, opened, self_mine, self_theirs, green, scratch=mix,
    )
    outer = third(False, open_outer, outer)
    beyond = row_above(outer)
    inner = third(True, open_inner, inner)
    beside = swapped(inner)
    open_outer, open_inner = run(
        part_body, (wide(n, n), wide(n, n)), [SM] * 3 + [VM] * 8, at, energies, energy_pair,
        outer_ham, inner_ham, mid, mid_turned, self_mine, self_theirs, outer, inner, scratch=mix,
    )
    whole_inner, keep_inner, give_inner = run(
        inner_body, (thin(n, n), thin(pairs, rows, n), thin(pairs, rows, n)), [SM] + [VM] * 4,
        at, near, open_inner, inner, beside, scratch=mix,
    )
    back_inner = [returned(whole_inner, True, slot) for slot in range(2)]
    got_inner = swapped(give_inner)
    whole_outer, chunks, give_outer = run(
        outer_body, (thin(n, n), thin(WIDTH, pairs, rows, n), thin(pairs, rows, n)), [SM] + [VM] * 6,
        at, far, open_outer, outer, beyond, keep_inner, got_inner, scratch=mix,
    )
    got_outer = swapped(give_outer)
    chunks = lax.dynamic_update_slice_in_dim(chunks, got_outer[None], 3 - 3 * core, 0)
    received = all_to_all(chunks.reshape(count, rows, n), ("x", "zlo", "y"))
    back_outer = [returned(whole_outer, False, slot) for slot in range(2)]
    result = convolved(received, strength, offsets, by_chip, natural)
    self_part = all_to_all(result.reshape(parts, 2, rows, n), ENERGY)
    green = run(spread_body, wide(2, n, n), [SM] + [VM] * 4, at, *back_inner, *back_outer)
    self_part = jnp.swapaxes(self_part, 0, 1).reshape(2, n, n)
    return (green[:, None], self_part[:, None])


def fine_mesh(mesh):
    energy, slab = mesh.shape["energy"], mesh.shape["slab"]
    zlo, y = (2, energy // 4) if energy > 2 else (1, 1)
    devices = mesh.devices.reshape(zlo, y, 2, slab // WIDTH, WIDTH)
    return jax.sharding.Mesh(devices, ("zlo", "y", "core", "row", "x"))


def solution(mesh):
    mesh = fine_mesh(mesh)
    return jax.shard_map(
        whole_run,
        mesh=mesh,
        in_specs=(P(ENERGY), P(SLAB), P(SLAB), P(SLAB, ENERGY), P()),
        out_specs=(P(ENERGY, SLAB), P(ENERGY, SLAB)),
        check_vma=False,
    )
```

```python
import functools

import jax
import jax.numpy as jnp
from jax import lax
from jax.experimental import pallas as pl
from jax.experimental.pallas import tpu as pltpu
from jax.sharding import PartitionSpec as P


BROAD = 0.3
REACH = 16

VM = pl.BlockSpec(memory_space=pltpu.VMEM)
SM = pl.BlockSpec(memory_space=pltpu.SMEM)


SLAB = ("row", "x")
ENERGY = ("zlo", "y", "core")
WIDTH = 4


def passed_along(value, steps):
    count = lax.axis_size(SLAB)
    leading, last = (max(0, -steps), min(count, count - steps))
    return lax.ppermute(value, SLAB, [(source, source + steps) for source in range(leading, last)])


def row_ring(value, steps):
    return lax.ppermute(value, "x", [(s, (s + steps) % WIDTH) for s in range(WIDTH)])


def row_step(value, steps):
    return lax.ppermute(value, "x", [(s, s + steps) for s in range(WIDTH) if 0 <= s + steps < WIDTH])


def swapped(value):
    return lax.ppermute(value, "core", [(0, 1), (1, 0)])


def row_above(value):
    rows = lax.axis_size("row")
    pairs = [(rows + r, r + 1) for r in range(rows - 1)] + [(r, rows + r - 1) for r in range(1, rows)]
    return lax.ppermute(value, ("core", "row"), pairs)


def crossed(value):
    rows = lax.axis_size("row")
    pairs = [(r * WIDTH - 1, r * WIDTH) for r in range(1, rows)]
    pairs += [(r * WIDTH, r * WIDTH - 1) for r in range(1, rows)]
    return lax.ppermute(value, ("core", "row", "x"), pairs)


def sent(value, pairs):
    return lax.ppermute(value, ("core", "x"), [(a * WIDTH + i, b * WIDTH + j) for (a, i), (b, j) in pairs])


def flipped(value, side):
    pairs = [(c * WIDTH + i, (i // 2) * WIDTH + 2 * c + (i % 2 + side) % 2) for c in range(2) for i in range(WIDTH)]
    return lax.ppermute(value, ("core", "x"), pairs)


def call(body, out_shape, in_specs, scratch=()):
    return pl.pallas_call(
        body,
        out_shape=out_shape,
        in_specs=in_specs,
        out_specs=jax.tree.map(lambda _: VM, out_shape),
        scratch_shapes=list(scratch),
        compiler_params=pltpu.CompilerParams(vmem_limit_bytes=16 * 1024 * 1024),
    )


def dot(a, b):
    return jnp.dot(a, b, preferred_element_type=jnp.float32)


def dot_t(a, b):
    return lax.dot_general(a, b, (((1,), (1,)), ((), ())), preferred_element_type=jnp.float32)


def tables(n):
    row = lax.broadcasted_iota(jnp.int32, (n, n), 0)
    col = lax.broadcasted_iota(jnp.int32, (n, n), 1)
    half = n // 2
    eye = jnp.where(row == col, 1.0, 0.0)
    rotate = jnp.where(col == row + half, -1.0, 0.0) + jnp.where(col == row - half, 1.0, 0.0)
    return eye, rotate


def own_body(keep_ref, at_ref, c_ref, ham_ref, own_ref, load_ref):
    own_ref[...] = dot_t(c_ref[...], c_ref[...]) * keep_ref[0]
    load_ref[...] = jnp.where(at_ref[0] == 0, ham_ref[...], c_ref[...])


def returned(value, inner, slot):
    pairs = []
    for c in range(2):
        block = (1 + c) if inner else 3 * c
        pairs += [(c * WIDTH + i, (i // 2) * WIDTH + block) for i in range(slot, WIDTH, 2)]
    return lax.ppermute(value, ("core", "x"), pairs)


def place_halves(core, whole, mine, theirs):
    half = mine.shape[0]
    whole[pl.ds(pl.multiple_of(core * half, half), half)] = mine
    whole[pl.ds(pl.multiple_of((1 - core) * half, half), half)] = theirs


def pair_body(at_ref, own_ref, mine_ref, theirs_ref, pair_ref, half_ref, below_ref, turned_ref):
    core = at_ref[0]
    half = half_ref.shape[0]
    place_halves(core, below_ref, mine_ref[...], theirs_ref[...])
    below = below_ref[...]
    turned = below.T
    turned_ref[...] = turned
    pair_ref[...] = own_ref[...] + dot(turned, below)
    half_ref[...] = pair_ref[pl.ds(pl.multiple_of(core * half, half), half)].astype(jnp.bfloat16)


def above_body(keep_ref, at_ref, c_ref, mine_ref, theirs_ref, out_ref, whole):
    place_halves(at_ref[0], whole, mine_ref[...], theirs_ref[...])
    out_ref[...] = dot_t(whole[...], whole[...]) * keep_ref[0] + dot(c_ref[...].T, c_ref[...])


def first_step(energy, inverse, ham, pair, eye):
    square = inverse * inverse
    return (
        (square * inverse) * pair.astype(jnp.float32) + square * ham + (2.0 * inverse - square * energy) * eye
    ).astype(jnp.bfloat16)


def linked(green, link):
    return dot(link, dot_t(green, link).astype(jnp.bfloat16))


def finish(matrix, green, eye):
    product = dot(matrix, green)
    residue = (2.0 * eye - product).astype(jnp.bfloat16)
    return dot(green, residue)


def near_body(at_ref, one_ref, three_ref, crossed_ref, previous_ref, next_ref):
    first = at_ref[0] == 0
    previous_ref[...] = jnp.where(jnp.logical_and(first, at_ref[1] == 0), crossed_ref[...], one_ref[...])
    next_ref[...] = jnp.where(jnp.logical_and(first, at_ref[1] == WIDTH - 1), crossed_ref[...], three_ref[...])


def second_body(
    energy_ref, inverse_ref, edge_ref, at_ref, ham_ref, pair_ref, c_ref, lower_turned_ref, previous_ref, next_ref,
    got_previous_ref, got_next_ref, above_ref, down_ref, got_down_ref, out_ref, first_ref, second_ref, whole,
):
    n = c_ref.shape[0]
    eye, rotate = tables(n)
    chunks = out_ref.shape[0]
    first = at_ref[0] == 0
    whole[0] = jnp.where(first, next_ref[...], got_next_ref[...])
    whole[1] = jnp.where(first, previous_ref[...], got_previous_ref[...])
    place_halves(at_ref[0], whole.at[2], down_ref[...], got_down_ref[...])
    odd = lax.rem(at_ref[1], 2)
    turn = BROAD * rotate
    ham = ham_ref[...].astype(jnp.float32) - turn
    ham_above = whole[0].astype(jnp.float32) - turn
    ham_below = whole[1].astype(jnp.float32) - turn
    for e, same_ref in ((odd, first_ref), (1 - odd, second_ref)):
        energy, inverse = energy_ref[e], inverse_ref[e]
        above = first_step(energy, inverse * edge_ref[0], ham_above, above_ref[...], eye)
        below = first_step(energy, inverse * edge_ref[1], ham_below, whole[2], eye)
        green = first_step(energy, inverse, ham, pair_ref[...], eye)
        terms = linked(above, c_ref[...]) + linked(below, lower_turned_ref[...])
        matrix = (energy * eye - ham - terms).astype(jnp.bfloat16)
        result = finish(matrix, green, eye).astype(jnp.bfloat16)
        out_ref[:, e] = result.reshape(chunks, n // chunks, n)
        same_ref[...] = result


def link_body(
    at_ref, c_ref, ham_ref, below_ref, spread_0, spread_1, spread_2, mine_1, mine_2, mine_3, other_1, other_2, other_3,
    outer_ham, inner_ham, far, mid, mid_turned, near,
):
    x = at_ref[1]

    def block(b, here, one, two, three):
        k = lax.rem(x + WIDTH - b, WIDTH)
        return jnp.where(k == 0, here, jnp.where(k == 1, one, jnp.where(k == 2, two, three)))

    @pl.when(at_ref[0] == 0)
    def _():
        end = x == WIDTH - 1
        hams = (ham_ref[...], mine_1[...], mine_2[...], jnp.where(end, spread_2[...], mine_3[...]))
        links = (c_ref[...], other_1[...], other_2[...], jnp.where(end, spread_1[...], other_3[...]))
        outer_ham[...] = block(0, *hams)
        inner_ham[...] = block(1, *hams)
        far[...] = jnp.where(x == 0, below_ref[...], jnp.where(x == 2, spread_1[...], spread_0[...])).T
        middle = block(0, *links)
        mid[...] = middle
        mid_turned[...] = middle.T
        near[...] = block(1, *links)

    @pl.when(at_ref[0] == 1)
    def _():
        hams = (ham_ref[...], jnp.where(x == 0, spread_0[...], other_1[...]), other_2[...], other_3[...])
        links = (c_ref[...], jnp.where(x == 0, spread_1[...], mine_1[...]), mine_2[...], mine_3[...])
        outer_ham[...] = block(3, *hams)
        inner_ham[...] = block(2, *hams)
        far[...] = block(3, *links)
        middle = block(2, *links)
        mid[...] = middle.T
        mid_turned[...] = middle
        near[...] = block(1, *links).T


def row_energy(at_ref, energy_ref, pair_ref):
    core, x = at_ref[0], at_ref[1]
    return jnp.where(x // 2 == core, energy_ref[lax.rem(x, 2)], pair_ref[lax.rem(x, 2)])


def role_body(at_ref, first_ref, second_ref, outer_ref, inner_ref):
    match = lax.rem(at_ref[1], 2) == at_ref[0]
    outer_ref[...] = jnp.where(match, first_ref[...], second_ref[...])
    inner_ref[...] = jnp.where(match, second_ref[...], first_ref[...])


def open_body(
    at_ref, energy_ref, energy_pair_ref, outer_ham, inner_ham, far, mid, mid_turned, near, outer, inner, beyond, beside, open_outer, open_inner,
):
    eye, rotate = tables(outer.shape[0])
    base = row_energy(at_ref, energy_ref, energy_pair_ref) * eye + BROAD * rotate
    open_outer[...] = (
        base - outer_ham[...].astype(jnp.float32) - linked(inner[...], mid[...]) - linked(beyond[...], far[...])
    )
    open_inner[...] = (
        base - inner_ham[...].astype(jnp.float32) - linked(outer[...], mid_turned[...]) - linked(beside[...], near[...])
    )


def joined_rows(core, slot, mine_ref, theirs_ref, scratch):
    scratch[:, core] = mine_ref[2 * core + slot]
    scratch[:, 1 - core] = theirs_ref[slot]
    n = scratch.shape[-1]
    return scratch[...].reshape(n, n).astype(jnp.float32)


def third_body(inner, at_ref, open_ref, mine_ref, theirs_ref, green_ref, out_ref, scratch):
    core = at_ref[0]
    eye, _ = tables(open_ref.shape[0])
    self_part = joined_rows(core, 1 - core if inner else core, mine_ref, theirs_ref, scratch)
    matrix = (open_ref[...] - self_part).astype(jnp.bfloat16)
    out_ref[...] = finish(matrix, green_ref[...], eye).astype(jnp.bfloat16)


def split_rows(core, result, keep_ref, give_ref, scratch):
    scratch[...] = result.reshape(scratch.shape)
    keep_ref[...] = scratch[:, core]
    give_ref[...] = scratch[:, 1 - core]


def part_body(
    at_ref, energy_ref, energy_pair_ref, outer_ham, inner_ham, mid, mid_turned, mine_ref, theirs_ref, outer, inner,
    open_outer, open_inner, scratch,
):
    core = at_ref[0]
    eye, rotate = tables(outer.shape[0])
    base = row_energy(at_ref, energy_ref, energy_pair_ref) * eye + BROAD * rotate
    self_part = joined_rows(core, 1 - core, mine_ref, theirs_ref, scratch)
    open_inner[...] = base - inner_ham[...].astype(jnp.float32) - self_part - linked(outer[...], mid_turned[...])
    self_part = joined_rows(core, core, mine_ref, theirs_ref, scratch)
    open_outer[...] = base - outer_ham[...].astype(jnp.float32) - self_part - linked(inner[...], mid[...])


def inner_body(at_ref, near, open_ref, inner, beside, whole_ref, keep_ref, give_ref, scratch):
    eye, _ = tables(inner.shape[0])
    matrix = (open_ref[...] - linked(beside[...], near[...])).astype(jnp.bfloat16)
    result = finish(matrix, inner[...], eye).astype(jnp.bfloat16)
    whole_ref[...] = result
    split_rows(at_ref[0], result, keep_ref, give_ref, scratch)


def outer_body(
    at_ref, far, open_ref, outer, beyond, keep_inner, got_inner, whole_ref, out_ref, give_ref, scratch
):
    core = at_ref[0]
    eye, _ = tables(outer.shape[0])
    matrix = (open_ref[...] - linked(beyond[...], far[...])).astype(jnp.bfloat16)
    result = finish(matrix, outer[...], eye).astype(jnp.bfloat16)
    whole_ref[...] = result
    scratch[...] = result.reshape(scratch.shape)
    give_ref[...] = scratch[:, 1 - core]
    out_ref[3 * core] = scratch[:, core]
    out_ref[1 + core] = keep_inner[...]
    out_ref[2 - core] = got_inner[...]
    out_ref[3 - 3 * core] = got_inner[...]


def spread_body(at_ref, inner_0, inner_1, outer_0, outer_1, out_ref):
    within = jnp.logical_and(at_ref[1] > 0, at_ref[1] < WIDTH - 1)
    out_ref[0] = jnp.where(within, inner_0[...], outer_0[...]).astype(jnp.float32)
    out_ref[1] = jnp.where(within, inner_1[...], outer_1[...]).astype(jnp.float32)


def energy_body(place_in, place_out, offset_ref, green_ref, coulomb_ref, out_ref, padded):
    count, rows, columns = green_ref.shape
    offset_count = offset_ref.shape[0]
    none = jnp.zeros((REACH, 8, 128), jnp.float32)
    padded[:REACH] = none
    padded[REACH + count :] = none
    column_tiles = columns // 128

    def tile(t, carry):
        row = pl.ds(pl.multiple_of(8 * (t // column_tiles), 8), 8)
        column = pl.ds(pl.multiple_of(128 * (t % column_tiles), 128), 128)
        strength = coulomb_ref[row, column].astype(jnp.float32)
        own = [green_ref[place_in[e], row, column].astype(jnp.float32) for e in range(count)]
        for e in range(count):
            padded[REACH + e] = own[e]
        screened = []
        for k in range(offset_count):
            later = padded.at[pl.ds(REACH + offset_ref[k], count)]
            sums = [own[e] * later[e] for e in range(4)]
            for e in range(4, count):
                sums[e % 4] = sums[e % 4] + own[e] * later[e]
            polarization = (4.0 / count) * ((sums[0] + sums[1]) + (sums[2] + sums[3]))
            screened.append(strength * (1.0 + polarization * strength) * (1.0 / offset_count))
        earlier = [padded.at[pl.ds(REACH - offset_ref[k], count)] for k in range(offset_count)]
        for e in range(count):
            terms = [screened[k] * earlier[k][e] for k in range(offset_count)]
            while len(terms) > 1:
                terms = [a + b for a, b in zip(terms[::2], terms[1::2])] + terms[len(terms) // 2 * 2 :]
            out_ref[place_out[e], row, column] = terms[0].astype(jnp.bfloat16)
        return carry

    lax.fori_loop(0, (rows // 8) * column_tiles, tile, 0)


def convolved(received, coulomb, offsets, place_in, place_out):
    count, rows, columns = received.shape
    return call(
        functools.partial(energy_body, place_in, place_out),
        jax.ShapeDtypeStruct((count, rows, columns), jnp.bfloat16),
        [SM, VM, VM],
        [pltpu.VMEM((count + 2 * REACH, 8, 128), jnp.float32)],
    )(offsets, received, coulomb)


def all_to_all(value, axes):
    return lax.all_to_all(value, axes, split_axis=0, concat_axis=0, tiled=True)


def whole_run(energies, hamiltonian, coupling, coulomb, offsets):
    c, ham, strength = coupling[0], hamiltonian[0], coulomb[0]
    n = c.shape[0]
    parts = lax.axis_size(ENERGY)
    rows, pairs = n // parts, parts // 2
    count = 2 * parts
    place, x, core = lax.axis_index(SLAB), lax.axis_index("x"), lax.axis_index("core")
    edge = jnp.stack([place < lax.axis_size(SLAB) - 1, place > 0, place < lax.axis_size(SLAB) - 2]).astype(jnp.float32)
    at = jnp.stack([core, x]).astype(jnp.int32)
    inverse = (1.0 / energies).astype(jnp.bfloat16).astype(jnp.float32)
    half = lambda value: lax.dynamic_slice_in_dim(value, core * (n // 2), n // 2, 0)
    wide = lambda *dims: jax.ShapeDtypeStruct(dims, jnp.float32)
    thin = lambda *dims: jax.ShapeDtypeStruct(dims, jnp.bfloat16)
    natural = list(range(count))
    by_chip = [(e % WIDTH) * (count // WIDTH) + e // WIDTH for e in range(count)]

    def run(body, out_shape, in_specs, *operands, scratch=()):
        return call(body, out_shape, in_specs, scratch)(*operands)

    c_half = half(c)
    lower_mine = passed_along(c_half, 1)
    upper_mine = passed_along(c_half, -1)
    energy_pair = swapped(energies)
    own, load = run(own_body, (wide(n, n), thin(n, n)), [SM, SM, VM, VM], edge[:1], at, c, ham)
    lower_theirs = swapped(lower_mine)
    one, three = row_step(load, 1), row_step(load, -1)
    crossing = crossed(ham)
    pair, pair_half, below_c, lower_turned = run(
        pair_body, (wide(n, n), thin(n // 2, n), thin(n, n), thin(n, n)), [SM, VM, VM, VM],
        at, own, lower_mine, lower_theirs,
    )
    pair_down = passed_along(pair_half, 1)
    upper_theirs = swapped(upper_mine)
    above = run(
        above_body, wide(n, n), [SM, SM, VM, VM, VM], edge[2:], at, c, upper_mine, upper_theirs,
        scratch=[pltpu.VMEM((n, n), jnp.bfloat16)],
    )
    two = row_ring(load, 2)
    before, after = run(near_body, (thin(n, n),) * 2, [SM] + [VM] * 3, at, one, three, crossing)
    got_before, got_after = swapped(before), swapped(after)
    got_down = swapped(pair_down)
    chunks, first, second = run(
        second_body, (thin(parts, 2, rows, n), thin(n, n), thin(n, n)), [SM] * 4 + [VM] * 11,
        energies, inverse, edge, at, ham, pair, c, lower_turned, before, after, got_before, got_after,
        above, pair_down, got_down, scratch=[pltpu.VMEM((3, n, n), jnp.bfloat16)],
    )
    first, second = flipped(first, 0), flipped(second, 1)
    received = all_to_all(chunks, ENERGY)

    got_two = swapped(two)
    starts = jnp.where(x == 0, below_c, load), jnp.where(jnp.logical_and(x == 0, core == 0), below_c, load), load
    routes = (
        [((0, 0), (0, 1)), ((1, 0), (0, 3)), ((0, 3), (1, 0))],
        [((0, 0), (0, 2)), ((1, 0), (0, 3)), ((1, 3), (1, 0))],
        [((0, 0), (0, 3))],
    )
    spread = [sent(value, route) for value, route in zip(starts, routes)]
    outer_ham, inner_ham, far, mid, mid_turned, near = run(
        link_body, (thin(n, n),) * 6, [SM] + [VM] * 12,
        at, c, ham, below_c, *spread, one, two, three, got_before, got_two, got_after,
    )
    outer, inner = run(role_body, (thin(n, n),) * 2, [SM, VM, VM], at, first, second)
    beyond = row_above(outer)
    beside = swapped(inner)
    open_outer, open_inner = run(
        open_body, (wide(n, n),) * 2, [SM] * 3 + [VM] * 10,
        at, energies, energy_pair, outer_ham, inner_ham, far, mid, mid_turned, near, outer, inner, beyond, beside,
    )
    result = convolved(received.reshape(count, rows, n), strength, offsets, natural, by_chip)
    self_mine = all_to_all(result, ("x", "zlo", "y")).reshape(WIDTH, pairs, rows, n)
    self_theirs = swapped(lax.dynamic_slice_in_dim(self_mine, 2 * (1 - core), 2, 0))
    mix = [pltpu.VMEM((pairs, 2, rows, n), jnp.bfloat16)]
    third = lambda role, opened, green: run(
        functools.partial(third_body, role), thin(n, n), [SM] + [VM] * 4,
        at, opened, self_mine, self_theirs, green, scratch=mix,
    )
    outer = third(False, open_outer, outer)
    beyond = row_above(outer)
    inner = third(True, open_inner, inner)
    beside = swapped(inner)
    open_outer, open_inner = run(
        part_body, (wide(n, n), wide(n, n)), [SM] * 3 + [VM] * 8, at, energies, energy_pair,
        outer_ham, inner_ham, mid, mid_turned, self_mine, self_theirs, outer, inner, scratch=mix,
    )
    whole_inner, keep_inner, give_inner = run(
        inner_body, (thin(n, n), thin(pairs, rows, n), thin(pairs, rows, n)), [SM] + [VM] * 4,
        at, near, open_inner, inner, beside, scratch=mix,
    )
    back_inner = [returned(whole_inner, True, slot) for slot in range(2)]
    got_inner = swapped(give_inner)
    whole_outer, chunks, give_outer = run(
        outer_body, (thin(n, n), thin(WIDTH, pairs, rows, n), thin(pairs, rows, n)), [SM] + [VM] * 6,
        at, far, open_outer, outer, beyond, keep_inner, got_inner, scratch=mix,
    )
    got_outer = swapped(give_outer)
    chunks = lax.dynamic_update_slice_in_dim(chunks, got_outer[None], 3 - 3 * core, 0)
    received = all_to_all(chunks.reshape(count, rows, n), ("x", "zlo", "y"))
    back_outer = [returned(whole_outer, False, slot) for slot in range(2)]
    result = convolved(received, strength, offsets, by_chip, natural)
    self_part = all_to_all(result.reshape(parts, 2, rows, n), ENERGY)
    green = run(spread_body, wide(2, n, n), [SM] + [VM] * 4, at, *back_inner, *back_outer)
    self_part = jnp.swapaxes(self_part, 0, 1).reshape(2, n, n)
    return (green[:, None], self_part[:, None])


def fine_mesh(mesh):
    energy, slab = mesh.shape["energy"], mesh.shape["slab"]
    zlo, y = (2, energy // 4) if energy > 2 else (1, 1)
    devices = mesh.devices.reshape(zlo, y, 2, slab // WIDTH, WIDTH)
    return jax.sharding.Mesh(devices, ("zlo", "y", "core", "row", "x"))


def solution(mesh):
    mesh = fine_mesh(mesh)
    return jax.shard_map(
        whole_run,
        mesh=mesh,
        in_specs=(P(ENERGY), P(SLAB), P(SLAB), P(SLAB, ENERGY), P()),
        out_specs=(P(ENERGY, SLAB), P(ENERGY, SLAB)),
        check_vma=False,
    )
```
